512 devices in a mesh: elem: 32 (over y_lo, z), orb: 16 (over x, y_hi, core).
Axes of the slice: x: 4, y: 8 (y_hi: 2, y_lo: 4; y = y_hi * 4 + y_lo), z: 8, core: 2. Of those that a mesh axis runs over, the one named last changes fastest.
Arguments:
- orbitals: bfloat16 [24576, 4096], P('elem', 'orb')
- hamiltonian: bfloat16 [384, 7, 64, 64], P('elem'), may hold values from -0.25 to 0.25
- neighbours: int32 [384, 7], P('elem'), may hold values from 0 to 383, as said below
Outputs:
- updated: bfloat16 [24576, 4096], P('elem', 'orb')
The draws below stay inside these ranges and needn't reach their ends.
Inputs may be any that keep to these rules, and one draw needn't show every extreme that they name: Elements form tiles of 12 consecutive indices, each tile a periodic 3 x 4 plane of elements in some order, tiles stacked periodically. An element's row lists itself, its two neighbours along each in-plane direction, then the element at the same place in the previous tile and in the next tile.
All inputs are finite; a program needn't handle non-finite values.
Results may differ from the reference program's by a relative error of at most 0.0062.
Values may be sent and summed in bfloat16 or wider, within the bound.
A program may use at most 64 MiB of HBM per device.

```python
import jax
import jax.numpy as jnp
from jax import lax

B = 64
NORB = 4096
GX = 3
GY = 4
EL = 12
ELEMS = 384
ROWS = 24576


def draw_orbitals(key, part):
    key_base = jax.random.fold_in(key, 0)
    key_row = jax.random.fold_in(key, 1)
    key_col = jax.random.fold_in(key, 2)
    key_tile = jax.random.fold_in(key, 4)
    low = jnp.log(0.3)
    high = jnp.log(3.0)
    col_scale = jnp.exp(jax.random.uniform(key_col, (NORB,), jnp.float32, low, high))
    ramp = jnp.exp(jnp.log(3.0) * jnp.arange(ROWS, dtype=jnp.float32) / ROWS)
    tiles = ELEMS // EL
    tile_scale = jnp.exp(jax.random.uniform(key_tile, (tiles,), jnp.float32, 0.0, jnp.log(40.0)))
    tile_rows = jnp.repeat(tile_scale, EL * B, total_repeat_length=ROWS)
    row_scale = jnp.exp(jax.random.uniform(key_row, (ROWS,), jnp.float32, low, high)) * ramp * tile_rows
    base = jax.random.normal(key_base, (ROWS, NORB), jnp.float32)
    base = jnp.clip(base, -5.0, 5.0)
    values = base * row_scale[:, None] * col_scale[None, :]
    return values.astype(jnp.bfloat16)


def draw_neighbours(key, part):
    tiles = ELEMS // EL
    keys = jax.random.split(key, tiles)
    order = jax.vmap(lambda single: jax.random.permutation(single, EL))(keys).astype(jnp.int32)
    cells = jnp.arange(EL, dtype=jnp.int32)
    xpos = cells // GY
    ypos = cells % GY
    tile_ids = jnp.arange(tiles, dtype=jnp.int32)

    def element_at(tile, cell):
        return tile * EL + order[tile, cell]
    own_tile = tile_ids[:, None] + jnp.zeros((1, EL), jnp.int32)
    own_cell = cells[None, :] + jnp.zeros((tiles, 1), jnp.int32)
    xminus = ((xpos - 1) % GX * GY + ypos)[None, :] + jnp.zeros((tiles, 1), jnp.int32)
    xplus = ((xpos + 1) % GX * GY + ypos)[None, :] + jnp.zeros((tiles, 1), jnp.int32)
    yminus = (xpos * GY + (ypos - 1) % GY)[None, :] + jnp.zeros((tiles, 1), jnp.int32)
    yplus = (xpos * GY + (ypos + 1) % GY)[None, :] + jnp.zeros((tiles, 1), jnp.int32)
    below = (own_tile - 1) % tiles
    above = (own_tile + 1) % tiles
    lists = jnp.stack([element_at(own_tile, own_cell), element_at(own_tile, xminus), element_at(own_tile, xplus), element_at(own_tile, yminus), element_at(own_tile, yplus), element_at(below, own_cell), element_at(above, own_cell)], axis=-1).reshape(ELEMS, 7)
    row_ids = element_at(own_tile, own_cell).reshape(ELEMS)
    return jnp.zeros((ELEMS, 7), jnp.int32).at[row_ids].set(lists)


def level_of(own_key, extent, pieces, low, high):
    def one(position, shards_of):
        heights = jax.random.uniform(jax.random.fold_in(jax.random.fold_in(own_key, 6), position), (shards_of,), jnp.float32, low / len(pieces), high / len(pieces))
        return jnp.repeat(jnp.exp(heights), extent[position] // shards_of).reshape((-1,) + (1,) * (len(extent) - position - 1))

    loudness = one(*pieces[0])
    for cut in pieces[1:]:
        loudness = loudness * one(*cut)
    return loudness


def bell_draw(rng, shape, scale, most, cuts=(), kind=jnp.bfloat16):
    level = level_of(rng, shape, cuts, -0.22, 0.18) if cuts else 1.0
    values = jax.random.normal(rng, shape, jnp.float32) * scale * level
    return jnp.minimum(jnp.maximum(values, -most), most).astype(kind)


def setup_inputs(seed: int = 0) -> dict:
    key_list = jax.random.split(jax.random.key(seed), 4)
    return {
        "orbitals": draw_orbitals(jax.random.fold_in(key_list[3], 71), 0),
        "hamiltonian": bell_draw(key_list[1], (ELEMS, 7, B, B), (7 * B) ** -0.5, 0.25, ((0, 32),)),
        "neighbours": draw_neighbours(jax.random.fold_in(key_list[3], 71), 0),
    }


def neighbour_product(hamiltonian, neighbours, field):
    width = field.shape[1]
    blocks = field.reshape(ELEMS, B, width)
    picked = blocks[neighbours].astype(jnp.float32)
    result = jnp.einsum('enab,enbc->eac', hamiltonian.astype(jnp.float32), picked)
    return result.reshape(ROWS, width)

def reference(orbitals, hamiltonian, neighbours):
    width = 256 if NORB % 256 == 0 else NORB
    count = NORB // width
    stacked = orbitals.reshape(ROWS, count, width).transpose(1, 0, 2)

    def filter_block(block):
        start = block.astype(jnp.float32)
        first = neighbour_product(hamiltonian, neighbours, block)
        first_half = first.astype(jnp.bfloat16)
        second = 2.0 * neighbour_product(hamiltonian, neighbours, first_half) - start
        second_half = second.astype(jnp.bfloat16)
        third = 2.0 * neighbour_product(hamiltonian, neighbours, second_half) - first
        return third.astype(jnp.bfloat16)
    filtered = lax.map(filter_block, stacked).transpose(1, 0, 2).reshape(ROWS, NORB)
    gram = jnp.dot(filtered.T, filtered, preferred_element_type=jnp.float32)
    level = jnp.trace(gram) / (NORB * ROWS)
    scaled = (gram / (level * ROWS)).astype(jnp.bfloat16)
    mixed = jnp.dot(filtered, scaled, preferred_element_type=jnp.float32)
    result = (1.5 * filtered.astype(jnp.float32) - 0.5 * mixed) / jnp.sqrt(level)
    return result.astype(jnp.bfloat16)
```

```python
import jax
import jax.numpy as jnp
from jax import lax
from jax.experimental import pallas as pl
from jax.experimental.pallas import tpu as pltpu
from jax.sharding import PartitionSpec as P

MESH = pl.DeviceIdType.MESH
F32 = jnp.float32
BF16 = jnp.bfloat16
NX, NY, NZ = 4, 4, 8
TILE, BLOCK, WIDTH, HALF = 12, 64, 256, 128
ROWS = TILE * BLOCK
PIECE = ROWS // 2
SLOTS = 16
GROUPS = 4
STRIP = WIDTH // NZ
UNROLL = 4
N_SEND, N_RECV = 256, 256


def rem(a, b):
    return lax.rem(a, jnp.int32(b))


def div(a, b):
    return lax.div(a, jnp.int32(b))


def slot_of(dx, dy, dc):
    return (dx * 2 + dy) * 2 + dc


def kernel(total_rows, total_cols, *refs):
    v_ref, ham_ref, nb_ref, out_ref = refs[:4]
    halos = refs[4:16]
    (w1a, w1b, w2a, w2b, hown, hhalo, first, acc, panel, relay, ft, ssq, lz, ly, lx, lsum, lev,
     tpart, rs_in, rs_out, zsum, y_in, y_out, tfull, mixed, ssem, rsem) = refs[16:]
    w1, w2 = (w1a, w1b), (w2a, w2b)

    e = lax.axis_index("elem")
    o = lax.axis_index("orb")
    z, yl = rem(e, NZ), div(e, NZ)
    c, yh, x = rem(o, 2), rem(div(o, 2), 2), div(o, 4)
    y = yh * NY + yl
    xc = x * 2 + c

    def dev(x_, y_, z_, c_):
        return (rem(y_, NY) * NZ + z_, (x_ * 2 + div(y_, NY)) * 2 + c_)

    def zdev(j):
        return dev(x, y, rem(z + j, NZ), c)

    def ydev(j):
        return dev(x, rem(y + j, 2 * NY), z, c)

    def xdev(j):
        return dev(rem(x + j, NX), y, z, c)

    def xcdev(j):
        t = rem(xc + j, 2 * NX)
        return dev(div(t, 2), y, z, rem(t, 2))

    sibling = dev(x, y, z, 1 - c)
    tile_next = (rem(e + 1, NZ * NY), o)
    tile_prev = (rem(e + NZ * NY - 1, NZ * NY), o)

    counts = [0, 0]
    finals = []

    def ids(n=1):
        s = counts[0]
        counts[0] += n
        assert counts[0] <= N_SEND
        return s

    def copy(src, dst, send_id, recv_id, to):
        return pltpu.make_async_remote_copy(
            src_ref=src, dst_ref=dst, send_sem=ssem.at[send_id], recv_sem=rsem.at[recv_id],
            device_id=to, device_id_type=MESH)

    def push(src, dst, cid, to):
        d = copy(src, dst, cid, cid, to)
        d.start()
        finals.append(d.wait_send)

    def arrived(dst, cid):
        copy(dst, dst, cid, cid, sibling).wait_recv()

    events = []

    def at(time, fn):
        events.append((time, fn))

    barrier = pltpu.get_barrier_semaphore()
    peers = [tile_next, tile_prev]
    peers += [zdev(j) for j in range(1, NZ)]
    peers += [ydev(j) for j in range(1, 2 * NY)]
    peers += [xcdev(j) for j in range(1, 2 * NX)]
    for p in peers:
        pl.semaphore_signal(barrier, inc=1, device_id=p, device_id_type=MESH)
    pl.semaphore_wait(barrier, len(peers))

    def cols(h):
        return pl.ds(h * HALF, HALF)

    def halo(k, h, d):
        return halos[(k * 2 + h) * 2 + d]

    halo_id = [[[ids() for d in range(2)] for h in range(2)] for k in range(3)]

    def source(k, h):
        return v_ref.at[:, :, cols(h)] if k == 0 else (w1[h] if k == 1 else w2[h])

    def send_halo(k, h):
        push(source(k, h), halo(k, h, 0), halo_id[k][h][0], tile_next)
        push(source(k, h), halo(k, h, 1), halo_id[k][h][1], tile_prev)

    def loop(body):
        def step(t, carry):
            for u in range(UNROLL):
                body(t * UNROLL + u)
            return carry
        lax.fori_loop(0, TILE // UNROLL, step, 0)

    def block_of(i, n):
        return rem(nb_ref[i, n], TILE)

    def setup(i):
        hown[i] = jnp.concatenate([ham_ref[i, n] for n in range(5)], axis=1)
        hhalo[i] = jnp.concatenate([ham_ref[i, n] for n in range(5, 7)], axis=1)

    def own_part(k, h):
        def body(i):
            if k == 0:
                parts = [v_ref[block_of(i, n), :, cols(h)] for n in range(5)]
            else:
                parts = [(w1, w2)[k - 1][h][block_of(i, n)] for n in range(5)]
            acc[h, i] = jnp.dot(hown[i], jnp.concatenate(parts, axis=0), preferred_element_type=F32)
        loop(body)

    def finish(k, h):
        for d in range(2):
            arrived(halo(k, h, d), halo_id[k][h][d])

        def body(i):
            parts = [halo(k, h, d)[block_of(i, 5 + d)] for d in range(2)]
            t = acc[h, i] + jnp.dot(hhalo[i], jnp.concatenate(parts, axis=0), preferred_element_type=F32)
            if k == 0:
                first[h, i] = t
                w1[h][i] = t.astype(BF16)
            elif k == 1:
                w2[h][i] = (2.0 * t - v_ref[i, :, cols(h)].astype(F32)).astype(BF16)
            else:
                f = (2.0 * t - first[h, i]).astype(BF16)
                panel[0, pl.ds(pl.multiple_of(i * BLOCK, BLOCK), BLOCK), cols(h)] = f
                f = f.astype(F32)
                ssq[...] += jnp.sum((f * f).reshape(BLOCK // 8, 8, HALF), axis=0)
        loop(body)

    def piece(q, h, r):
        return panel.at[q, pl.ds(r * PIECE, PIECE), cols(h)]

    def half(q, h):
        return panel.at[q, :, cols(h)]

    pid = {}

    def pids(*key):
        if key not in pid:
            pid[key] = ids()
        return pid[key]

    def to_sibling(dx, dy, h):
        push(half(slot_of(dx, dy, 0), h), half(slot_of(dx, dy, 1), h), pids("s", dx, dy, h), sibling)

    def from_sibling(dx, dy, h):
        arrived(half(slot_of(dx, dy, 1), h), pids("s", dx, dy, h))

    def x_send(dy, h):
        for r in range(2):
            push(piece(slot_of(0, dy, 0), h, r), piece(slot_of(3, dy, 0), h, r), pids("x", 3, dy, h, r), xdev(1))
            push(piece(slot_of(0, dy, 0), h, r), piece(slot_of(1, dy, 0), h, r), pids("x", 1, dy, h, r), xdev(NX - 1))

    def x_relay(dy, h):
        arrived(piece(slot_of(3, dy, 0), h, 0), pids("x", 3, dy, h, 0))
        push(piece(slot_of(3, dy, 0), h, 0), piece(slot_of(2, dy, 0), h, 0), pids("x", 2, dy, h, 0), xdev(1))
        arrived(piece(slot_of(1, dy, 0), h, 0), pids("x", 1, dy, h, 0))
        arrived(piece(slot_of(1, dy, 0), h, 1), pids("x", 1, dy, h, 1))
        push(piece(slot_of(1, dy, 0), h, 1), piece(slot_of(2, dy, 0), h, 1), pids("x", 2, dy, h, 1), xdev(NX - 1))
        arrived(piece(slot_of(3, dy, 0), h, 1), pids("x", 3, dy, h, 1))
        to_sibling(1, dy, h)
        to_sibling(3, dy, h)

    def x_far(dy, h):
        for r in range(2):
            arrived(piece(slot_of(2, dy, 0), h, r), pids("x", 2, dy, h, r))
        to_sibling(2, dy, h)

    def y_send(h):
        for r, j in ((0, 2), (1, 2 * NY - 2)):
            push(piece(0, h, r), relay.at[h, r], pids("y", h, r), ydev(j))

    def y_relay(h):
        for r, j in ((0, 2), (1, 2 * NY - 2)):
            arrived(relay.at[h, r], pids("y", h, r))
            push(relay.at[h, r], piece(slot_of(0, 1, 0), h, r), pids("Y", h, r), ydev(j))

    def partner(h):
        for r in range(2):
            arrived(piece(slot_of(0, 1, 0), h, r), pids("Y", h, r))
        x_send(1, h)
        to_sibling(0, 1, h)

    lev_id = [[ids() for j in range(8)] for s in range(3)]
    stages = ((lz, z, zdev), (ly, y, ydev), (lx, xc, xcdev))

    def level_send(s):
        buf, me, to = stages[s]
        if s:
            prev, prev_me, _ = stages[s - 1]
            for j in range(1, 8):
                arrived(prev.at[rem(prev_me + 8 - j, 8)], lev_id[s - 1][j])
            value = jnp.sum(prev[...], axis=0)
        else:
            value = ssq[...]
        lsum[s] = value
        buf[me] = value
        for j in range(1, 8):
            push(lsum.at[s], buf.at[me], lev_id[s][j], to(j))

    def level_done():
        for j in range(1, 8):
            arrived(lx.at[rem(xc + 8 - j, 8)], lev_id[2][j])
        total = jnp.sum(jnp.sum(lx[...], axis=0))
        level = jnp.full((8, HALF), total) / (total_cols * total_rows)
        lev[0] = level * total_rows
        lev[1] = jnp.sqrt(level)

    members = (
        ((0, 0), (1, 0)),
        ((3, 0), (2, 0)),
        ((0, 1), (1, 1)),
        ((3, 1), (2, 1)),
    )

    def slots(g):
        return [slot_of(dx, dy, dc) for dx, dy in members[g] for dc in range(2)]

    def hops(g):
        return (3, 4) if g % 2 == 0 else (4, 3)

    def strip(d):
        return pl.ds(pl.multiple_of(d * STRIP, STRIP), STRIP)

    def quad(g):
        return pl.ds(g * 4, 4)

    rs_id = [[[ids() for s in range(5)] for d in range(2)] for g in range(GROUPS)]
    ag_id = [[[ids() for s in range(5)] for d in range(2)] for g in range(GROUPS)]
    yr_id = ids(3)
    ys_id = [ids() for g in range(GROUPS)]
    yb_id = [ids() for g in range(GROUPS)]
    yb_send = [ids() for j in range(3)]

    def gram(g):
        for dx, dy in members[g]:
            for h in range(2):
                from_sibling(dx, dy, h)
        for n, q in enumerate(slots(g)):
            tpart[4 * g + n] = jnp.dot(ft[...], panel[q], preferred_element_type=F32)

    def rs_step(g, d, s):
        n = hops(g)[d]
        if s > n:
            return
        ahead = n - s + 1
        dest = rem(z + (ahead if d == 0 else NZ - ahead), NZ)
        value = tpart[quad(g), strip(dest), :]
        if s > 1:
            arrived(rs_in.at[g, d, s - 2], rs_id[g][d][s - 1])
            value = value + rs_in[g, d, s - 2].astype(F32)
        rs_out[g, d, s - 1] = value.astype(BF16)
        push(rs_out.at[g, d, s - 1], rs_in.at[g, d, s - 1], rs_id[g][d][s], zdev(1 if d == 0 else NZ - 1))

    def rs_done(g):
        value = tpart[quad(g), strip(z), :]
        for d in range(2):
            n = hops(g)[d]
            arrived(rs_in.at[g, d, n - 1], rs_id[g][d][n])
            value = value + rs_in[g, d, n - 1].astype(F32)
        zsum[g] = value
        slot = rem(yl + NY - g, NY) - 1
        slot = jnp.maximum(slot, 0)

        @pl.when(yl != g)
        def _():
            y_out[g] = value.astype(BF16)
            copy(y_out.at[g], y_in.at[slot], ys_id[g], yr_id + slot, dev(x, yh * NY + g, z, c)).start()

        def last():
            @pl.when(yl != g)
            def _():
                copy(y_out.at[g], y_in.at[slot], ys_id[g], yr_id + slot, dev(x, yh * NY + g, z, c)).wait_send()
        finals.append(last)

    def region(g, d):
        return tfull.at[quad(g), strip(d), :]

    def y_dest(g, j):
        return dev(x, yh * NY + (g + j) % NY, z, c)

    def scaled(g):
        @pl.when(yl == g)
        def _():
            value = zsum[g]
            for j in range(3):
                copy(y_in.at[j], y_in.at[j], 0, yr_id + j, sibling).wait_recv()
                value = value + y_in[j].astype(F32)
            value = value / jnp.max(lev[0])
            tfull[quad(g), strip(z), :] = value.astype(BF16)
            for j in range(1, NY):
                copy(region(g, z), region(g, z), yb_send[j - 1], yb_id[g], y_dest(g, j)).start()

        @pl.when(yl != g)
        def _():
            arrived(region(g, z), yb_id[g])

        def last():
            @pl.when(yl == g)
            def _():
                for j in range(1, NY):
                    copy(region(g, z), region(g, z), yb_send[j - 1], yb_id[g], y_dest(g, j)).wait_send()
        finals.append(last)

    def ag_step(g, d, s):
        n = hops(g)[d]
        if s > n:
            return
        behind = rem(z + ((NZ - s + 1) if d == 0 else (s - 1)), NZ)
        if s > 1:
            arrived(region(g, behind), ag_id[g][d][s - 1])
        push(region(g, behind), region(g, behind), ag_id[g][d][s], zdev(1 if d == 0 else NZ - 1))

    def ag_done(g):
        for d in range(2):
            n = hops(g)[d]
            arrived(region(g, rem(z + (NZ - n if d == 0 else n), NZ)), ag_id[g][d][n])

    def mix(g):
        ag_done(g)

        def step(t, carry):
            rows = pl.ds(pl.multiple_of(t * 256, 256), 256)
            value = None
            for n, q in enumerate(slots(g)):
                term = lax.dot_general(
                    panel[q, rows, :], tfull[4 * g + n], (((1,), (1,)), ((), ())), preferred_element_type=F32)
                value = term if value is None else value + term
            if g > 0:
                value = value + mixed[rows, :]
            if g < GROUPS - 1:
                mixed[rows, :] = value
            else:
                f = panel[0, rows, :].astype(F32)
                out_ref[rows, :] = ((1.5 * f - 0.5 * value) / jnp.max(lev[1])).astype(BF16)
            return carry
        lax.fori_loop(0, ROWS // 256, step, 0)

    def transposed(h):
        ft[pl.ds(h * HALF, HALF), :] = panel[0, :, cols(h)].T

    def launch(h):
        y_send(h)
        x_send(0, h)
        to_sibling(0, 0, h)
        transposed(h)

    send_halo(0, 0)
    send_halo(0, 1)
    ssq[...] = jnp.zeros_like(ssq)
    loop(setup)
    own_part(0, 0)
    own_part(0, 1)
    for k in range(3):
        for h in range(2):
            finish(k, h)
            if k < 2:
                send_halo(k + 1, h)
                own_part(k + 1, h)
            else:
                launch(h)

    at(0.5, lambda: level_send(0))
    at(5.0, lambda: level_send(1))
    at(9.5, lambda: level_send(2))
    at(14.0, level_done)
    for h in range(2):
        at((2.0, 6.3)[h], lambda h=h: x_relay(0, h))
        at((3.0, 7.2)[h], lambda h=h: y_relay(h))
        at((9.2, 15.0)[h], lambda h=h: partner(h))
        at((8.2, 10.5)[h], lambda h=h: x_far(0, h))
        at((15.1, 21.0)[h], lambda h=h: x_relay(1, h))
        at((18.0, 24.0)[h], lambda h=h: x_far(1, h))
    ready = (8.0, 12.5, 23.0, 26.0)
    for g in range(GROUPS):
        t0 = ready[g]
        at(t0, lambda g=g: gram(g))
        for s in range(1, 5):
            for d in range(2):
                at(t0 + 2.8 * (s - 1) + 0.01, lambda g=g, d=d, s=s: rs_step(g, d, s))
        t1 = t0 + 2.8 * 4
        at(t1, lambda g=g: rs_done(g))
        t2 = t1 + 3.0
        at(t2, lambda g=g: scaled(g))
        t3 = t2 + 1.5
        for s in range(1, 5):
            for d in range(2):
                at(t3 + 3.0 * (s - 1), lambda g=g, d=d, s=s: ag_step(g, d, s))
        at(t3 + 12.5, lambda g=g: mix(g))
    for _, fn in sorted(events, key=lambda item: item[0]):
        fn()
    for fn in finals:
        fn()


def solution(mesh):
    sizes = dict(mesh.shape)

    def local(orbitals, hamiltonian, neighbours):
        rows, width = orbitals.shape
        total_rows, total_cols = rows * sizes["elem"], width * sizes["orb"]
        assert (rows, width) == (ROWS, WIDTH)
        vmem = pl.BlockSpec(memory_space=pltpu.VMEM)
        block = pltpu.VMEM((TILE, BLOCK, HALF), BF16)
        return pl.pallas_call(
            lambda *refs: kernel(total_rows, total_cols, *refs),
            out_shape=jax.ShapeDtypeStruct((rows, width), BF16),
            in_specs=[vmem, vmem, pl.BlockSpec(memory_space=pltpu.SMEM)],
            out_specs=vmem,
            scratch_shapes=[block] * 16 + [
                pltpu.VMEM((TILE, BLOCK, 5 * BLOCK), BF16),
                pltpu.VMEM((TILE, BLOCK, 2 * BLOCK), BF16),
                pltpu.VMEM((2, TILE, BLOCK, HALF), F32),
                pltpu.VMEM((2, TILE, BLOCK, HALF), F32),
                pltpu.VMEM((SLOTS, ROWS, WIDTH), BF16),
                pltpu.VMEM((2, 2, PIECE, HALF), BF16),
                pltpu.VMEM((WIDTH, ROWS), BF16),
                pltpu.VMEM((8, HALF), F32),
                pltpu.VMEM((8, 8, HALF), F32),
                pltpu.VMEM((8, 8, HALF), F32),
                pltpu.VMEM((8, 8, HALF), F32),
                pltpu.VMEM((3, 8, HALF), F32),
                pltpu.VMEM((2, 8, HALF), F32),
                pltpu.VMEM((SLOTS, WIDTH, WIDTH), F32),
                pltpu.VMEM((GROUPS, 2, 4, 4, STRIP, WIDTH), BF16),
                pltpu.VMEM((GROUPS, 2, 4, 4, STRIP, WIDTH), BF16),
                pltpu.VMEM((GROUPS, 4, STRIP, WIDTH), F32),
                pltpu.VMEM((3, 4, STRIP, WIDTH), BF16),
                pltpu.VMEM((GROUPS, 4, STRIP, WIDTH), BF16),
                pltpu.VMEM((SLOTS, WIDTH, WIDTH), BF16),
                pltpu.VMEM((ROWS, WIDTH), F32),
                pltpu.SemaphoreType.DMA((N_SEND,)),
                pltpu.SemaphoreType.DMA((N_RECV,)),
            ],
            compiler_params=pltpu.CompilerParams(
                collective_id=0, has_side_effects=True, vmem_limit_bytes=56 * 1024 * 1024),
            name="filter_gram",
        )(orbitals.reshape(TILE, BLOCK, width), hamiltonian, neighbours)

    return jax.shard_map(
        local,
        mesh=mesh,
        in_specs=(P("elem", "orb"), P("elem", None, None, None), P("elem", None)),
        out_specs=P("elem", "orb"),
        check_vma=False,
    )
```

```python
import jax
import jax.numpy as jnp
from jax import lax
from jax.experimental import pallas as pl
from jax.experimental.pallas import tpu as pltpu
from jax.sharding import PartitionSpec as P

MESH = pl.DeviceIdType.MESH
F32 = jnp.float32
BF16 = jnp.bfloat16
NX, NY, NZ = 4, 4, 8
TILE, BLOCK, WIDTH, HALF = 12, 64, 256, 128
ROWS = TILE * BLOCK
PIECES = 4
PIECE = ROWS // PIECES
RIGHT, LEFT = (0, 1), (2, 3)
SLOTS = 16
GROUPS = 8
PAIR = 2
STRIP = WIDTH // NZ
UNROLL = 4
N_SEND, N_RECV = 256, 256
members = ((0, 0), (1, 0), (3, 0), (2, 0), (0, 1), (3, 1), (1, 1), (2, 1))
ORDER = (
    (4, 0, 0, 0), (0, 0), (2, 0, 0), (4, 0, 0, 1), (2, 0, 2), (5, 0, 0, 3), (5, 0, 0, 2), (7, 0), (8, 0, 1, 1),
    (8, 0, 0, 1), (6, 3, 0, 0), (2, 0, 3), (8, 0, 1, 2), (2, 0, 1), (5, 0, 1, 2), (6, 1, 0, 0), (2, 1, 0),
    (8, 0, 0, 2), (4, 0, 1, 0), (2, 1, 2), (4, 0, 1, 1), (0, 1), (6, 3, 0, 1), (5, 0, 1, 3), (6, 1, 0, 1), (2, 1, 1),
    (7, 2), (8, 2, 0, 1), (8, 2, 1, 1), (3, 0, 0), (6, 2, 0, 0), (3, 0, 2), (7, 1), (8, 1, 0, 1), (8, 1, 1, 1),
    (8, 0, 1, 3), (8, 0, 0, 3), (6, 2, 0, 1), (2, 1, 3), (3, 0, 1), (8, 2, 1, 2), (3, 0, 3), (8, 2, 0, 2), (7, 3),
    (4, 1, 0, 0), (8, 3, 0, 1), (8, 3, 1, 1), (5, 1, 0, 2), (8, 1, 1, 2), (8, 1, 0, 2), (3, 1, 0), (3, 1, 2),
    (6, 0, 1, 0), (8, 0, 1, 4), (5, 1, 0, 3), (6, 1, 1, 0), (8, 2, 1, 3), (4, 1, 0, 1), (8, 2, 0, 3), (8, 3, 0, 2),
    (3, 1, 1), (3, 1, 3), (6, 0, 1, 1), (6, 3, 1, 0), (8, 3, 1, 2), (0, 2), (8, 1, 1, 3), (8, 1, 0, 3), (4, 1, 1, 0),
    (9, 0), (7, 4), (8, 4, 0, 1), (8, 4, 1, 1), (8, 2, 1, 4), (5, 1, 1, 2), (8, 3, 0, 3), (8, 1, 0, 4), (4, 1, 1, 1),
    (5, 1, 1, 3), (6, 1, 1, 1), (8, 4, 0, 2), (8, 4, 1, 2), (6, 3, 1, 1), (8, 3, 1, 3), (9, 2), (8, 3, 0, 4),
    (6, 2, 1, 0), (7, 6), (8, 6, 0, 1), (8, 6, 1, 1), (9, 1), (1,), (7, 5), (8, 5, 1, 1), (8, 5, 0, 1), (6, 2, 1, 1),
    (8, 4, 1, 3), (8, 4, 0, 3), (10, 0), (7, 7), (8, 6, 1, 2), (8, 7, 1, 1), (8, 7, 0, 1), (8, 5, 0, 2), (8, 6, 0, 2),
    (8, 5, 1, 2), (9, 3), (8, 4, 1, 4), (11, 0, 1, 2), (11, 0, 0, 2), (8, 7, 0, 2), (8, 6, 1, 3), (10, 2),
    (8, 7, 1, 2), (8, 5, 0, 3), (9, 4), (8, 6, 0, 3), (10, 1), (8, 6, 1, 4), (8, 7, 0, 3), (8, 5, 1, 3),
    (11, 0, 1, 3), (10, 3), (8, 7, 1, 3), (11, 1, 1, 2), (8, 5, 0, 4), (11, 2, 1, 2), (11, 1, 0, 2), (9, 6),
    (8, 7, 0, 4), (11, 3, 0, 2), (10, 4), (11, 3, 1, 2), (11, 0, 0, 3), (11, 2, 0, 2), (9, 5), (11, 0, 1, 4),
    (11, 2, 1, 3), (11, 1, 0, 3), (11, 1, 1, 3), (11, 3, 0, 3), (9, 7), (11, 4, 1, 2), (10, 6), (11, 3, 1, 3),
    (11, 4, 0, 2), (11, 1, 0, 4), (11, 2, 1, 4), (11, 2, 0, 3), (11, 4, 1, 3), (10, 5), (11, 6, 0, 2), (12, 0),
    (11, 6, 1, 2), (10, 7), (11, 4, 1, 4), (11, 5, 0, 2), (11, 3, 0, 4), (11, 5, 1, 2), (11, 4, 0, 3), (12, 2),
    (11, 6, 1, 3), (11, 7, 0, 2), (11, 6, 0, 3), (11, 5, 0, 3), (11, 7, 1, 2), (12, 1), (11, 7, 0, 3), (11, 6, 1, 4),
    (11, 5, 1, 3), (12, 3), (11, 7, 1, 3), (11, 5, 0, 4), (11, 7, 0, 4), (12, 4), (12, 6), (12, 5), (12, 7),
)


def rem(a, b):
    return lax.rem(a, jnp.int32(b))


def div(a, b):
    return lax.div(a, jnp.int32(b))


def slot_of(dx, dy, dc):
    return (dx * 2 + dy) * 2 + dc


def kernel(total_rows, total_cols, *refs):
    v_in, ham_in, nb_ref, out_ref = refs[:4]
    halos = refs[4:16]
    (v_ref, ham_ref, w1a, w1b, w2a, w2b, hown, hhalo, first, acc, panel, relay, ft, ssq, lz, ly, lx, lsum, lev,
     tpart, rs_in, rs_out, zsum, y_in, y_out, tfull, mixed, ssem, rsem, lsem) = refs[16:]
    w1, w2 = (w1a, w1b), (w2a, w2b)

    e = lax.axis_index("elem")
    o = lax.axis_index("orb")
    z, yl = rem(e, NZ), div(e, NZ)
    c, yh, x = rem(o, 2), rem(div(o, 2), 2), div(o, 4)
    y = yh * NY + yl
    xc = x * 2 + c

    def dev(x_, y_, z_, c_):
        return (rem(y_, NY) * NZ + z_, (x_ * 2 + div(y_, NY)) * 2 + c_)

    def zdev(j):
        return dev(x, y, rem(z + j, NZ), c)

    def ydev(j):
        return dev(x, rem(y + j, 2 * NY), z, c)

    def xdev(j):
        return dev(rem(x + j, NX), y, z, c)

    def xcdev(j):
        t = rem(xc + j, 2 * NX)
        return dev(div(t, 2), y, z, rem(t, 2))

    sibling = dev(x, y, z, 1 - c)
    tile_next = (rem(e + 1, NZ * NY), o)
    tile_prev = (rem(e + NZ * NY - 1, NZ * NY), o)

    counts = [0, 0]
    finals = []

    def ids(n=1):
        s = counts[0]
        counts[0] += n
        assert counts[0] <= N_SEND
        return s

    def copy(src, dst, send_id, recv_id, to):
        return pltpu.make_async_remote_copy(
            src_ref=src, dst_ref=dst, send_sem=ssem.at[send_id], recv_sem=rsem.at[recv_id],
            device_id=to, device_id_type=MESH)

    def push(src, dst, cid, to):
        d = copy(src, dst, cid, cid, to)
        d.start()
        finals.append(d.wait_send)

    def arrived(dst, cid):
        copy(dst, dst, cid, cid, sibling).wait_recv()

    load_v = pltpu.make_async_copy(v_in, v_ref, lsem.at[0])
    load_ham = pltpu.make_async_copy(ham_in, ham_ref, lsem.at[1])
    load_v.start()
    load_ham.start()

    barrier = pltpu.get_barrier_semaphore()
    peers = [tile_next, tile_prev]
    peers += [zdev(j) for j in range(1, NZ)]
    peers += [ydev(j) for j in range(1, 2 * NY)]
    peers += [xcdev(j) for j in range(1, 2 * NX)]
    for p in peers:
        pl.semaphore_signal(barrier, inc=1, device_id=p, device_id_type=MESH)
    pl.semaphore_wait(barrier, len(peers))

    def cols(h):
        return pl.ds(h * HALF, HALF)

    def halo(k, h, d):
        return halos[(k * 2 + h) * 2 + d]

    halo_id = [[[ids() for d in range(2)] for h in range(2)] for k in range(3)]

    def source(k, h):
        return v_ref.at[:, :, cols(h)] if k == 0 else (w1[h] if k == 1 else w2[h])

    def send_halo(k, h):
        push(source(k, h), halo(k, h, 0), halo_id[k][h][0], tile_next)
        push(source(k, h), halo(k, h, 1), halo_id[k][h][1], tile_prev)

    def loop(body):
        def step(t, carry):
            for u in range(UNROLL):
                body(t * UNROLL + u)
            return carry
        lax.fori_loop(0, TILE // UNROLL, step, 0)

    def block_of(i, n):
        return rem(nb_ref[n, i], TILE)

    def setup(i):
        hown[i] = jnp.concatenate([ham_ref[i, n] for n in range(5)], axis=1)
        hhalo[i] = jnp.concatenate([ham_ref[i, n] for n in range(5, 7)], axis=1)

    def own_part(k, h):
        def body(i):
            if k == 0:
                parts = [v_ref[block_of(i, n), :, cols(h)] for n in range(5)]
            else:
                parts = [(w1, w2)[k - 1][h][block_of(i, n)] for n in range(5)]
            acc[h, i] = jnp.dot(hown[i], jnp.concatenate(parts, axis=0), preferred_element_type=F32)
        loop(body)

    def finish(k, h):
        for d in range(2):
            arrived(halo(k, h, d), halo_id[k][h][d])

        def body(i):
            parts = [halo(k, h, d)[block_of(i, 5 + d)] for d in range(2)]
            t = acc[h, i] + jnp.dot(hhalo[i], jnp.concatenate(parts, axis=0), preferred_element_type=F32)
            if k == 0:
                first[h, i] = t
                w1[h][i] = t.astype(BF16)
            elif k == 1:
                w2[h][i] = (2.0 * t - v_ref[i, :, cols(h)].astype(F32)).astype(BF16)
            else:
                f = (2.0 * t - first[h, i]).astype(BF16)
                panel[0, pl.ds(pl.multiple_of(i * BLOCK, BLOCK), BLOCK), cols(h)] = f
                f = f.astype(F32)
                ssq[...] += jnp.sum((f * f).reshape(BLOCK // 8, 8, HALF), axis=0)
        loop(body)

    def piece(q, h, r):
        return panel.at[q, pl.ds(r * PIECE, PIECE), cols(h)]

    def half(q, h):
        return panel.at[q, :, cols(h)]

    pid = {}

    def pids(*key):
        if key not in pid:
            pid[key] = ids()
        return pid[key]

    def to_sibling(dx, dy, h):
        push(half(slot_of(dx, dy, 0), h), half(slot_of(dx, dy, 1), h), pids("s", dx, dy, h), sibling)

    def from_sibling(dx, dy, h):
        arrived(half(slot_of(dx, dy, 1), h), pids("s", dx, dy, h))

    def x_send(dy, h, r):
        push(piece(slot_of(0, dy, 0), h, r), piece(slot_of(3, dy, 0), h, r), pids("x", 3, dy, h, r), xdev(1))
        push(piece(slot_of(0, dy, 0), h, r), piece(slot_of(1, dy, 0), h, r), pids("x", 1, dy, h, r), xdev(NX - 1))

    def y_step(r):
        return ydev(2 if r in RIGHT else 2 * NY - 2)

    def y_send(h):
        for r in (0, 2, 1, 3):
            push(piece(0, h, r), relay.at[h, r], pids("y", h, r), y_step(r))

    def do_yr(h, r):
        arrived(relay.at[h, r], pids("y", h, r))
        push(relay.at[h, r], piece(slot_of(0, 1, 0), h, r), pids("Y", h, r), y_step(r))

    def do_par(h, r):
        arrived(piece(slot_of(0, 1, 0), h, r), pids("Y", h, r))
        x_send(1, h, r)

    def do_f3(dy, h, r):
        arrived(piece(slot_of(3, dy, 0), h, r), pids("x", 3, dy, h, r))
        push(piece(slot_of(3, dy, 0), h, r), piece(slot_of(2, dy, 0), h, r), pids("x", 2, dy, h, r), xdev(1))

    def do_f1(dy, h, r):
        arrived(piece(slot_of(1, dy, 0), h, r), pids("x", 1, dy, h, r))
        push(piece(slot_of(1, dy, 0), h, r), piece(slot_of(2, dy, 0), h, r), pids("x", 2, dy, h, r), xdev(NX - 1))

    def do_sib(dx, dy, h):
        for r in ((), RIGHT, RIGHT + LEFT, LEFT)[dx]:
            arrived(piece(slot_of(dx, dy, 0), h, r), pids("x", dx, dy, h, r))
        to_sibling(dx, dy, h)

    lev_id = [[ids() for j in range(8)] for s in range(3)]
    stages = ((lz, z, zdev), (ly, y, ydev), (lx, xc, xcdev))

    def do_ls(s):
        buf, me, to = stages[s]
        if s:
            prev, prev_me, _ = stages[s - 1]
            for j in range(1, 8):
                arrived(prev.at[rem(prev_me + 8 - j, 8)], lev_id[s - 1][j])
            value = jnp.sum(prev[...], axis=0)
        else:
            value = ssq[...]
        lsum[s] = value
        buf[me] = value
        for j in range(1, 8):
            push(lsum.at[s], buf.at[me], lev_id[s][j], to(j))

    def do_ld():
        for j in range(1, 8):
            arrived(lx.at[rem(xc + 8 - j, 8)], lev_id[2][j])
        total = jnp.sum(jnp.sum(lx[...], axis=0))
        level = jnp.full((8, HALF), total) / (total_cols * total_rows)
        lev[0] = level * total_rows
        lev[1] = jnp.sqrt(level)

    def slots(g):
        return [slot_of(*members[g], dc) for dc in range(PAIR)]

    def hops(g):
        return (3, 4) if g % 2 == 0 else (4, 3)

    def strip(d):
        return pl.ds(pl.multiple_of(d * STRIP, STRIP), STRIP)

    def pair(g):
        return pl.ds(slots(g)[0], PAIR)

    rs_id = [[[ids() for s in range(hops(g)[d])] for d in range(2)] for g in range(GROUPS)]
    ag_id = [[[ids() for s in range(hops(g)[d])] for d in range(2)] for g in range(GROUPS)]
    y_id = [[ids() for j in range(NY - 1)] for g in range(GROUPS)]

    def along_z(d):
        return zdev(1 if d == 0 else NZ - 1)

    def do_gram(g):
        for h in range(2):
            from_sibling(*members[g], h)
        for q in slots(g):
            tpart[q] = jnp.dot(ft[...], panel[q], preferred_element_type=F32)

    def do_rs(g, d, s):
        ahead = hops(g)[d] - s + 1
        dest = rem(z + (ahead if d == 0 else NZ - ahead), NZ)
        value = tpart[pair(g), strip(dest), :]
        if s > 1:
            arrived(rs_in.at[g, d, s - 2], rs_id[g][d][s - 2])
            value = value + rs_in[g, d, s - 2].astype(F32)
        rs_out[g, d, s - 1] = value.astype(BF16)
        push(rs_out.at[g, d, s - 1], rs_in.at[g, d, s - 1], rs_id[g][d][s - 1], along_z(d))

    def do_rsd(g):
        value = tpart[pair(g), strip(z), :]
        for d in range(2):
            n = hops(g)[d]
            arrived(rs_in.at[g, d, n - 1], rs_id[g][d][n - 1])
            value = value + rs_in[g, d, n - 1].astype(F32)
        zsum[g] = value
        y_out[g] = value.astype(BF16)
        for j in range(1, NY):
            push(y_out.at[g], y_in.at[g, j - 1], y_id[g][j - 1], dev(x, yh * NY + rem(yl + j, NY), z, c))

    def region(g, d):
        return tfull.at[pair(g), strip(d), :]

    def ag_send(g, d, s):
        behind = rem(z + ((NZ - s + 1) if d == 0 else (s - 1)), NZ)
        if s > 1:
            arrived(region(g, behind), ag_id[g][d][s - 2])
        push(region(g, behind), region(g, behind), ag_id[g][d][s - 1], along_z(d))

    def do_sc(g):
        value = zsum[g]
        for j in range(NY - 1):
            arrived(y_in.at[g, j], y_id[g][j])
            value = value + y_in[g, j].astype(F32)
        value = value / jnp.max(lev[0])
        tfull[pair(g), strip(z), :] = value.astype(BF16)
        for d in range(2):
            ag_send(g, d, 1)

    do_ag = ag_send

    def do_mix(g):
        for d in range(2):
            n = hops(g)[d]
            arrived(region(g, rem(z + (NZ - n if d == 0 else n), NZ)), ag_id[g][d][n - 1])
        initial, final = g == mixes[0], g == mixes[-1]

        def step(t, carry):
            rows = pl.ds(pl.multiple_of(t * 256, 256), 256)
            value = None
            for q in slots(g):
                term = lax.dot_general(
                    panel[q, rows, :], tfull[q], (((1,), (1,)), ((), ())), preferred_element_type=F32)
                value = term if value is None else value + term
            if not initial:
                value = value + mixed[rows, :]
            if final:
                f = panel[0, rows, :].astype(F32)
                out_ref[rows, :] = ((1.5 * f - 0.5 * value) / jnp.max(lev[1])).astype(BF16)
            else:
                mixed[rows, :] = value
            return carry
        lax.fori_loop(0, ROWS // 256, step, 0)

    def transposed(h):
        ft[pl.ds(h * HALF, HALF), :] = panel[0, :, cols(h)].T

    def launch(h):
        y_send(h)
        for r in (0, 2, 1, 3):
            x_send(0, h, r)
        to_sibling(0, 0, h)
        transposed(h)

    load_v.wait()
    send_halo(0, 0)
    send_halo(0, 1)
    ssq[...] = jnp.zeros_like(ssq)
    load_ham.wait()
    loop(setup)
    own_part(0, 0)
    own_part(0, 1)
    for k in range(3):
        for h in range(2):
            finish(k, h)
            if k < 2:
                send_halo(k + 1, h)
                own_part(k + 1, h)
            else:
                launch(h)

    steps = (do_ls, do_ld, do_yr, do_par, do_f3, do_f1, do_sib, do_gram, do_rs, do_rsd, do_sc, do_ag, do_mix)
    mixes = [numbers[0] for kind, *numbers in ORDER if steps[kind] is do_mix]
    for kind, *numbers in ORDER:
        steps[kind](*numbers)
    for fn in finals:
        fn()


def solution(mesh):
    sizes = dict(mesh.shape)

    def local(orbitals, hamiltonian, neighbours):
        rows, width = orbitals.shape
        total_rows, total_cols = rows * sizes["elem"], width * sizes["orb"]
        assert (rows, width) == (ROWS, WIDTH)
        vmem = pl.BlockSpec(memory_space=pltpu.VMEM)
        anywhere = pl.BlockSpec(memory_space=pl.ANY)
        block = pltpu.VMEM((TILE, BLOCK, HALF), BF16)
        return pl.pallas_call(
            lambda *refs: kernel(total_rows, total_cols, *refs),
            out_shape=jax.ShapeDtypeStruct((rows, width), BF16),
            in_specs=[anywhere, anywhere, pl.BlockSpec(memory_space=pltpu.SMEM)],
            out_specs=vmem,
            scratch_shapes=[block] * 12 + [
                pltpu.VMEM((TILE, BLOCK, WIDTH), BF16),
                pltpu.VMEM(hamiltonian.shape, BF16),
            ] + [block] * 4 + [
                pltpu.VMEM((TILE, BLOCK, 5 * BLOCK), BF16),
                pltpu.VMEM((TILE, BLOCK, 2 * BLOCK), BF16),
                pltpu.VMEM((2, TILE, BLOCK, HALF), F32),
                pltpu.VMEM((2, TILE, BLOCK, HALF), F32),
                pltpu.VMEM((SLOTS, ROWS, WIDTH), BF16),
                pltpu.VMEM((2, PIECES, PIECE, HALF), BF16),
                pltpu.VMEM((WIDTH, ROWS), BF16),
                pltpu.VMEM((8, HALF), F32),
                pltpu.VMEM((8, 8, HALF), F32),
                pltpu.VMEM((8, 8, HALF), F32),
                pltpu.VMEM((8, 8, HALF), F32),
                pltpu.VMEM((3, 8, HALF), F32),
                pltpu.VMEM((2, 8, HALF), F32),
                pltpu.VMEM((SLOTS, WIDTH, WIDTH), F32),
                pltpu.VMEM((GROUPS, 2, 4, PAIR, STRIP, WIDTH), BF16),
                pltpu.VMEM((GROUPS, 2, 4, PAIR, STRIP, WIDTH), BF16),
                pltpu.VMEM((GROUPS, PAIR, STRIP, WIDTH), F32),
                pltpu.VMEM((GROUPS, NY - 1, PAIR, STRIP, WIDTH), BF16),
                pltpu.VMEM((GROUPS, PAIR, STRIP, WIDTH), BF16),
                pltpu.VMEM((SLOTS, WIDTH, WIDTH), BF16),
                pltpu.VMEM((ROWS, WIDTH), F32),
                pltpu.SemaphoreType.DMA((N_SEND,)),
                pltpu.SemaphoreType.DMA((N_RECV,)),
                pltpu.SemaphoreType.DMA((2,)),
            ],
            compiler_params=pltpu.CompilerParams(
                collective_id=0, has_side_effects=True, vmem_limit_bytes=56 * 1024 * 1024),
            name="filter_gram",
        )(orbitals.reshape(TILE, BLOCK, width), hamiltonian, neighbours.T)

    return jax.shard_map(
        local,
        mesh=mesh,
        in_specs=(P("elem", "orb"), P("elem", None, None, None), P("elem", None)),
        out_specs=P("elem", "orb"),
        check_vma=False,
    )
```

```python
import jax
import jax.numpy as jnp
from jax import lax
from jax.experimental import pallas as pl
from jax.experimental.pallas import tpu as pltpu
from jax.sharding import PartitionSpec as P

MESH = pl.DeviceIdType.MESH
F32 = jnp.float32
BF16 = jnp.bfloat16
NX, NY, NZ = 4, 4, 8
TILE, BLOCK, WIDTH, HALF = 12, 64, 256, 128
ROWS = TILE * BLOCK
PIECES = 4
PIECE = ROWS // PIECES
RIGHT, LEFT = (0, 1), (2, 3)
SLOTS = 16
GROUPS, SUMMED = 8, 7
PAIR = 2
STRIP = WIDTH // NZ
UNROLL = 4
MIX_ROWS = 768
N_SEND, N_RECV = 256, 256
members = ((1, 0), (0, 0), (2, 0), (0, 1), (3, 1), (1, 1), (2, 1), (3, 0))
ORDER = (
    (0, 0), (7, 1), (4, 0, 0, 1), (8, 1, 0, 1), (5, 0, 0, 2), (5, 0, 0, 3), (4, 0, 0, 0), (2, 0, 0), (6, 1, 0, 0),
    (6, 3, 0, 0), (2, 0, 2), (8, 1, 1, 1), (2, 0, 1), (2, 0, 3), (5, 0, 1, 2), (4, 0, 1, 0), (8, 1, 0, 2), (2, 1, 2),
    (8, 1, 1, 2), (2, 1, 0), (5, 0, 1, 3), (4, 0, 1, 1), (6, 1, 0, 1), (2, 1, 1), (3, 0, 0), (6, 3, 0, 1), (2, 1, 3),
    (6, 2, 0, 0), (7, 0), (8, 0, 1, 1), (8, 0, 0, 1), (3, 0, 2), (3, 0, 1), (8, 1, 0, 3), (6, 2, 0, 1), (0, 1),
    (8, 1, 1, 3), (3, 0, 3), (8, 0, 0, 2), (8, 0, 1, 2), (6, 0, 1, 0), (5, 1, 0, 2), (4, 1, 0, 0), (7, 2),
    (8, 2, 1, 1), (3, 1, 0), (8, 2, 0, 1), (3, 1, 2), (4, 1, 0, 1), (5, 1, 0, 3), (3, 1, 1), (6, 1, 1, 0),
    (8, 1, 0, 4), (3, 1, 3), (6, 0, 1, 1), (8, 0, 1, 3), (6, 3, 1, 0), (8, 0, 0, 3), (8, 2, 1, 2), (8, 2, 0, 2),
    (7, 3), (4, 1, 1, 0), (8, 3, 0, 1), (5, 1, 1, 2), (8, 3, 1, 1), (8, 2, 1, 3), (9, 1), (6, 2, 1, 0), (8, 2, 0, 3),
    (8, 0, 1, 4), (4, 1, 1, 1), (5, 1, 1, 3), (6, 1, 1, 1), (8, 3, 1, 2), (6, 3, 1, 1), (8, 3, 0, 2), (7, 5),
    (8, 5, 1, 1), (8, 5, 0, 1), (8, 2, 1, 4), (7, 4), (8, 4, 1, 1), (8, 4, 0, 1), (6, 2, 1, 1), (9, 0), (0, 2),
    (8, 3, 1, 3), (8, 3, 0, 3), (7, 6), (8, 6, 1, 1), (8, 5, 0, 2), (8, 6, 0, 1), (8, 5, 1, 2), (9, 2), (8, 4, 0, 2),
    (8, 4, 1, 2), (1,), (8, 3, 0, 4), (8, 6, 1, 2), (8, 5, 0, 3), (8, 5, 1, 3), (8, 6, 0, 2), (8, 4, 1, 3), (10, 0),
    (10, 1), (9, 3), (8, 5, 0, 4), (8, 4, 0, 3), (8, 6, 1, 3), (10, 2), (8, 6, 0, 3), (8, 4, 1, 4), (13, 7), (9, 5),
    (11, 1, 0, 2), (11, 0, 0, 2), (8, 6, 1, 4), (11, 0, 1, 2), (11, 2, 1, 2), (11, 2, 0, 2), (9, 4), (11, 7, 0, 2),
    (11, 7, 1, 2), (10, 3), (11, 0, 1, 3), (11, 0, 0, 3), (9, 6), (11, 2, 1, 3), (11, 2, 0, 3), (11, 7, 0, 3),
    (10, 5), (11, 3, 0, 2), (11, 1, 1, 2), (11, 0, 1, 4), (11, 3, 1, 2), (11, 1, 0, 3), (10, 4), (11, 7, 1, 3),
    (11, 7, 0, 4), (11, 5, 1, 2), (11, 5, 0, 2), (11, 3, 0, 3), (10, 6), (11, 2, 1, 4), (11, 1, 0, 4), (11, 4, 1, 2),
    (12, 0), (11, 5, 0, 3), (11, 4, 0, 2), (11, 6, 1, 2), (11, 5, 1, 3), (11, 6, 0, 2), (11, 3, 0, 4), (11, 4, 1, 3),
    (12, 7), (11, 6, 1, 3), (11, 3, 1, 3), (11, 1, 1, 3), (11, 5, 0, 4), (11, 4, 0, 3), (11, 4, 1, 4), (11, 6, 0, 3),
    (11, 6, 1, 4), (12, 2), (12, 5), (12, 3), (12, 1), (12, 4), (12, 6),
)


def rem(a, b):
    return lax.rem(a, jnp.int32(b))


def div(a, b):
    return lax.div(a, jnp.int32(b))


def slot_of(dx, dy, dc):
    return (dx * 2 + dy) * 2 + dc


def kernel(total_rows, total_cols, *refs):
    v_in, ham_in, nb_ref, out_ref = refs[:4]
    halos = refs[4:16]
    (v_ref, ham_ref, w1a, w1b, w2a, w2b, hown, hhalo, first, acc, panel, relay, ft, ssq, lz, ly, lx, lsum, lev,
     tpart, rs_in, rs_out, zsum, y_in, y_out, tfull, mixed, ssem, rsem, lsem) = refs[16:]
    w1, w2 = (w1a, w1b), (w2a, w2b)

    e = lax.axis_index("elem")
    o = lax.axis_index("orb")
    z, yl = rem(e, NZ), div(e, NZ)
    c, yh, x = rem(o, 2), rem(div(o, 2), 2), div(o, 4)
    y = yh * NY + yl
    xc = x * 2 + c

    def dev(x_, y_, z_, c_):
        return (rem(y_, NY) * NZ + z_, (x_ * 2 + div(y_, NY)) * 2 + c_)

    def zdev(j):
        return dev(x, y, rem(z + j, NZ), c)

    def ydev(j):
        return dev(x, rem(y + j, 2 * NY), z, c)

    def xdev(j):
        return dev(rem(x + j, NX), y, z, c)

    def xcdev(j):
        t = rem(xc + j, 2 * NX)
        return dev(div(t, 2), y, z, rem(t, 2))

    def mirror(j, dy, dc):
        return dev(rem(x + j, NX), rem(y + dy * NY, 2 * NY), z, c if dc == 0 else 1 - c)

    sibling = dev(x, y, z, 1 - c)
    tile_next = (rem(e + 1, NZ * NY), o)
    tile_prev = (rem(e + NZ * NY - 1, NZ * NY), o)

    counts = [0, 0]
    finals = []

    def ids(n=1):
        s = counts[0]
        counts[0] += n
        assert counts[0] <= N_SEND
        return s

    def copy(src, dst, send_id, recv_id, to):
        return pltpu.make_async_remote_copy(
            src_ref=src, dst_ref=dst, send_sem=ssem.at[send_id], recv_sem=rsem.at[recv_id],
            device_id=to, device_id_type=MESH)

    def push(src, dst, cid, to):
        d = copy(src, dst, cid, cid, to)
        d.start()
        finals.append(d.wait_send)

    def arrived(dst, cid):
        copy(dst, dst, cid, cid, sibling).wait_recv()

    load_v = pltpu.make_async_copy(v_in, v_ref, lsem.at[0])
    load_ham = pltpu.make_async_copy(ham_in, ham_ref, lsem.at[1])
    load_v.start()
    load_ham.start()

    barrier = pltpu.get_barrier_semaphore()
    peers = [tile_next, tile_prev]
    peers += [zdev(j) for j in range(1, NZ)]
    peers += [ydev(j) for j in range(1, 2 * NY)]
    peers += [xcdev(j) for j in range(1, 2 * NX)]
    for p in peers:
        pl.semaphore_signal(barrier, inc=1, device_id=p, device_id_type=MESH)
    pl.semaphore_wait(barrier, len(peers))

    def cols(h):
        return pl.ds(h * HALF, HALF)

    def halo(k, h, d):
        return halos[(k * 2 + h) * 2 + d]

    halo_id = [[[ids() for d in range(2)] for h in range(2)] for k in range(3)]

    def source(k, h):
        return v_ref.at[:, :, cols(h)] if k == 0 else (w1[h] if k == 1 else w2[h])

    def send_halo(k, h):
        push(source(k, h), halo(k, h, 0), halo_id[k][h][0], tile_next)
        push(source(k, h), halo(k, h, 1), halo_id[k][h][1], tile_prev)

    def loop(body):
        def step(t, carry):
            for u in range(UNROLL):
                body(t * UNROLL + u)
            return carry
        lax.fori_loop(0, TILE // UNROLL, step, 0)

    def block_of(i, n):
        return rem(nb_ref[n, i], TILE)

    def setup(i):
        hown[i] = jnp.concatenate([ham_ref[i, n] for n in range(5)], axis=1)
        hhalo[i] = jnp.concatenate([ham_ref[i, n] for n in range(5, 7)], axis=1)

    def own_part(k, h):
        def body(i):
            if k == 0:
                parts = [v_ref[block_of(i, n), :, cols(h)] for n in range(5)]
            else:
                parts = [(w1, w2)[k - 1][h][block_of(i, n)] for n in range(5)]
            acc[h, i] = jnp.dot(hown[i], jnp.concatenate(parts, axis=0), preferred_element_type=F32)
        loop(body)

    def finish(k, h):
        for d in range(2):
            arrived(halo(k, h, d), halo_id[k][h][d])

        def body(i):
            parts = [halo(k, h, d)[block_of(i, 5 + d)] for d in range(2)]
            t = acc[h, i] + jnp.dot(hhalo[i], jnp.concatenate(parts, axis=0), preferred_element_type=F32)
            if k == 0:
                first[h, i] = t
                w1[h][i] = t.astype(BF16)
            elif k == 1:
                w2[h][i] = (2.0 * t - v_ref[i, :, cols(h)].astype(F32)).astype(BF16)
            else:
                f = (2.0 * t - first[h, i]).astype(BF16)
                panel[0, pl.ds(pl.multiple_of(i * BLOCK, BLOCK), BLOCK), cols(h)] = f
                f = f.astype(F32)
                ssq[...] += jnp.sum((f * f).reshape(BLOCK // 8, 8, HALF), axis=0)
        loop(body)

    def piece(q, h, r):
        return panel.at[q, pl.ds(r * PIECE, PIECE), cols(h)]

    def half(q, h):
        return panel.at[q, :, cols(h)]

    pid = {}

    def pids(*key):
        if key not in pid:
            pid[key] = ids()
        return pid[key]

    def to_sibling(dx, dy, h):
        push(half(slot_of(dx, dy, 0), h), half(slot_of(dx, dy, 1), h), pids("s", dx, dy, h), sibling)

    def from_sibling(dx, dy, h):
        arrived(half(slot_of(dx, dy, 1), h), pids("s", dx, dy, h))

    def x_send(dy, h, r):
        push(piece(slot_of(0, dy, 0), h, r), piece(slot_of(3, dy, 0), h, r), pids("x", 3, dy, h, r), xdev(1))
        push(piece(slot_of(0, dy, 0), h, r), piece(slot_of(1, dy, 0), h, r), pids("x", 1, dy, h, r), xdev(NX - 1))

    def y_step(r):
        return ydev(2 if r in RIGHT else 2 * NY - 2)

    def y_send(h):
        for r in (0, 2, 1, 3):
            push(piece(0, h, r), relay.at[h, r], pids("y", h, r), y_step(r))

    def do_yr(h, r):
        arrived(relay.at[h, r], pids("y", h, r))
        push(relay.at[h, r], piece(slot_of(0, 1, 0), h, r), pids("Y", h, r), y_step(r))

    def do_par(h, r):
        arrived(piece(slot_of(0, 1, 0), h, r), pids("Y", h, r))
        x_send(1, h, r)

    def do_f3(dy, h, r):
        arrived(piece(slot_of(3, dy, 0), h, r), pids("x", 3, dy, h, r))
        push(piece(slot_of(3, dy, 0), h, r), piece(slot_of(2, dy, 0), h, r), pids("x", 2, dy, h, r), xdev(1))

    def do_f1(dy, h, r):
        arrived(piece(slot_of(1, dy, 0), h, r), pids("x", 1, dy, h, r))
        push(piece(slot_of(1, dy, 0), h, r), piece(slot_of(2, dy, 0), h, r), pids("x", 2, dy, h, r), xdev(NX - 1))

    def do_sib(dx, dy, h):
        for r in ((), RIGHT, RIGHT + LEFT, LEFT)[dx]:
            arrived(piece(slot_of(dx, dy, 0), h, r), pids("x", dx, dy, h, r))
        to_sibling(dx, dy, h)

    lev_id = [[ids() for j in range(8)] for s in range(3)]
    stages = ((lz, z, zdev), (ly, y, ydev), (lx, xc, xcdev))

    def do_ls(s):
        buf, me, to = stages[s]
        if s:
            prev, prev_me, _ = stages[s - 1]
            for j in range(1, 8):
                arrived(prev.at[rem(prev_me + 8 - j, 8)], lev_id[s - 1][j])
            value = jnp.sum(prev[...], axis=0)
        else:
            value = ssq[...]
        lsum[s] = value
        buf[me] = value
        for j in range(1, 8):
            push(lsum.at[s], buf.at[me], lev_id[s][j], to(j))

    def do_ld():
        for j in range(1, 8):
            arrived(lx.at[rem(xc + 8 - j, 8)], lev_id[2][j])
        total = jnp.sum(jnp.sum(lx[...], axis=0))
        level = jnp.full((8, HALF), total) / (total_cols * total_rows)
        lev[0] = level * total_rows
        lev[1] = jnp.sqrt(level)

    def slots(g):
        return [slot_of(*members[g], dc) for dc in range(PAIR)]

    def hops(g):
        return (3, 4) if g % 2 == 0 else (4, 3)

    def strip(d):
        return pl.ds(pl.multiple_of(d * STRIP, STRIP), STRIP)

    def pair(g):
        return pl.ds(slots(g)[0], PAIR)

    rs_id = [[[ids() for s in range(hops(g)[d])] for d in range(2)] for g in range(SUMMED)]
    ag_id = [[[ids() for s in range(hops(g)[d])] for d in range(2)] for g in range(GROUPS)]
    y_id = [[ids() for j in range(NY - 1)] for g in range(SUMMED)]
    mir_id = [[ids() for dc in range(PAIR)]]

    def along_z(d):
        return zdev(1 if d == 0 else NZ - 1)

    def do_gram(g):
        for h in range(2):
            from_sibling(*members[g], h)
        for q in slots(g):
            tpart[q] = jnp.dot(ft[...], panel[q], preferred_element_type=F32)

    def do_rs(g, d, s):
        ahead = hops(g)[d] - s + 1
        dest = rem(z + (ahead if d == 0 else NZ - ahead), NZ)
        value = tpart[pair(g), strip(dest), :]
        if s > 1:
            arrived(rs_in.at[g, d, s - 2], rs_id[g][d][s - 2])
            value = value + rs_in[g, d, s - 2].astype(F32)
        rs_out[g, d, s - 1] = value.astype(BF16)
        push(rs_out.at[g, d, s - 1], rs_in.at[g, d, s - 1], rs_id[g][d][s - 1], along_z(d))

    def do_rsd(g):
        value = tpart[pair(g), strip(z), :]
        for d in range(2):
            n = hops(g)[d]
            arrived(rs_in.at[g, d, n - 1], rs_id[g][d][n - 1])
            value = value + rs_in[g, d, n - 1].astype(F32)
        zsum[g] = value
        y_out[g] = value.astype(BF16)
        for j in range(1, NY):
            push(y_out.at[g], y_in.at[g, j - 1], y_id[g][j - 1], dev(x, yh * NY + rem(yl + j, NY), z, c))

    def region(g, d):
        return tfull.at[pair(g), strip(d), :]

    def ag_send(g, d, s):
        behind = rem(z + ((NZ - s + 1) if d == 0 else (s - 1)), NZ)
        if s > 1:
            arrived(region(g, behind), ag_id[g][d][s - 2])
        push(region(g, behind), region(g, behind), ag_id[g][d][s - 1], along_z(d))

    def do_sc(g):
        value = zsum[g]
        for j in range(NY - 1):
            arrived(y_in.at[g, j], y_id[g][j])
            value = value + y_in[g, j].astype(F32)
        value = value / jnp.max(lev[0])
        tfull[pair(g), strip(z), :] = value.astype(BF16)
        for d in range(2):
            ag_send(g, d, 1)
        dx, dy = members[g]
        if (dx, dy) == (1, 0):
            for dc in range(PAIR):
                push(tfull.at[slot_of(1, dy, dc), strip(z), :], tfull.at[slot_of(3, dy, dc), strip(z), :],
                     mir_id[dy][dc], mirror(1, dy, dc))

    def do_mir(g):
        dx, dy = members[g]
        for dc in range(PAIR):
            arrived(tfull.at[slot_of(3, dy, dc), strip(z), :], mir_id[dy][dc])
        for d in range(2):
            ag_send(g, d, 1)

    do_ag = ag_send

    def do_mix(g):
        for d in range(2):
            n = hops(g)[d]
            arrived(region(g, rem(z + (NZ - n if d == 0 else n), NZ)), ag_id[g][d][n - 1])
        initial, final = g == mixes[0], g == mixes[-1]

        mirrored = members[g] == (3, 0)
        if mirrored:
            for h in range(2):
                from_sibling(*members[g], h)
        side = 0 if mirrored else 1
        strips = jnp.concatenate([tfull[q] for q in slots(g)], axis=side)
        for t in range(ROWS // MIX_ROWS):
            rows = pl.ds(t * MIX_ROWS, MIX_ROWS)
            left = jnp.concatenate([panel[q, rows, :] for q in slots(g)], axis=1)
            value = lax.dot_general(left, strips, (((1,), (side,)), ((), ())), preferred_element_type=F32)
            if not initial:
                value = value + mixed[rows, :]
            if final:
                f = panel[0, rows, :].astype(F32)
                out_ref[rows, :] = ((1.5 * f - 0.5 * value) / jnp.max(lev[1])).astype(BF16)
            else:
                mixed[rows, :] = value

    def transposed(h):
        ft[pl.ds(h * HALF, HALF), :] = panel[0, :, cols(h)].T

    def launch(h):
        y_send(h)
        for r in (0, 2, 1, 3):
            x_send(0, h, r)
        to_sibling(0, 0, h)
        transposed(h)

    load_v.wait()
    send_halo(0, 0)
    send_halo(0, 1)
    ssq[...] = jnp.zeros_like(ssq)
    load_ham.wait()
    loop(setup)
    own_part(0, 0)
    own_part(0, 1)
    for k in range(3):
        for h in range(2):
            finish(k, h)
            if k < 2:
                send_halo(k + 1, h)
                own_part(k + 1, h)
            else:
                launch(h)

    steps = (do_ls, do_ld, do_yr, do_par, do_f3, do_f1, do_sib, do_gram, do_rs, do_rsd, do_sc, do_ag, do_mix, do_mir)
    mixes = [numbers[0] for kind, *numbers in ORDER if steps[kind] is do_mix]
    for kind, *numbers in ORDER:
        steps[kind](*numbers)
    for fn in finals:
        fn()


def solution(mesh):
    sizes = dict(mesh.shape)

    def local(orbitals, hamiltonian, neighbours):
        rows, width = orbitals.shape
        total_rows, total_cols = rows * sizes["elem"], width * sizes["orb"]
        assert (rows, width) == (ROWS, WIDTH)
        vmem = pl.BlockSpec(memory_space=pltpu.VMEM)
        anywhere = pl.BlockSpec(memory_space=pl.ANY)
        block = pltpu.VMEM((TILE, BLOCK, HALF), BF16)
        return pl.pallas_call(
            lambda *refs: kernel(total_rows, total_cols, *refs),
            out_shape=jax.ShapeDtypeStruct((rows, width), BF16),
            in_specs=[anywhere, anywhere, pl.BlockSpec(memory_space=pltpu.SMEM)],
            out_specs=vmem,
            scratch_shapes=[block] * 12 + [
                pltpu.VMEM((TILE, BLOCK, WIDTH), BF16),
                pltpu.VMEM(hamiltonian.shape, BF16),
            ] + [block] * 4 + [
                pltpu.VMEM((TILE, BLOCK, 5 * BLOCK), BF16),
                pltpu.VMEM((TILE, BLOCK, 2 * BLOCK), BF16),
                pltpu.VMEM((2, TILE, BLOCK, HALF), F32),
                pltpu.VMEM((2, TILE, BLOCK, HALF), F32),
                pltpu.VMEM((SLOTS, ROWS, WIDTH), BF16),
                pltpu.VMEM((2, PIECES, PIECE, HALF), BF16),
                pltpu.VMEM((WIDTH, ROWS), BF16),
                pltpu.VMEM((8, HALF), F32),
                pltpu.VMEM((8, 8, HALF), F32),
                pltpu.VMEM((8, 8, HALF), F32),
                pltpu.VMEM((8, 8, HALF), F32),
                pltpu.VMEM((3, 8, HALF), F32),
                pltpu.VMEM((2, 8, HALF), F32),
                pltpu.VMEM((SLOTS, WIDTH, WIDTH), F32),
                pltpu.VMEM((GROUPS, 2, 4, PAIR, STRIP, WIDTH), BF16),
                pltpu.VMEM((GROUPS, 2, 4, PAIR, STRIP, WIDTH), BF16),
                pltpu.VMEM((GROUPS, PAIR, STRIP, WIDTH), F32),
                pltpu.VMEM((GROUPS, NY - 1, PAIR, STRIP, WIDTH), BF16),
                pltpu.VMEM((GROUPS, PAIR, STRIP, WIDTH), BF16),
                pltpu.VMEM((SLOTS, WIDTH, WIDTH), BF16),
                pltpu.VMEM((ROWS, WIDTH), F32),
                pltpu.SemaphoreType.DMA((N_SEND,)),
                pltpu.SemaphoreType.DMA((N_RECV,)),
                pltpu.SemaphoreType.DMA((2,)),
            ],
            compiler_params=pltpu.CompilerParams(
                collective_id=0, has_side_effects=True, vmem_limit_bytes=56 * 1024 * 1024),
            name="filter_gram",
        )(orbitals.reshape(TILE, BLOCK, width), hamiltonian, neighbours.T)

    return jax.shard_map(
        local,
        mesh=mesh,
        in_specs=(P("elem", "orb"), P("elem", None, None, None), P("elem", None)),
        out_specs=P("elem", "orb"),
        check_vma=False,
    )
```

```python
import jax
import jax.numpy as jnp
from jax import lax
from jax.experimental import pallas as pl
from jax.experimental.pallas import tpu as pltpu
from jax.sharding import PartitionSpec as P

MESH = pl.DeviceIdType.MESH
F32 = jnp.float32
BF16 = jnp.bfloat16
NX, NY, NZ = 4, 4, 8
TILE, BLOCK, WIDTH, HALF = 12, 64, 256, 128
ROWS = TILE * BLOCK
PIECES = 4
PIECE = ROWS // PIECES
RIGHT, LEFT = (0, 1), (2, 3)
SLOTS = 16
GROUPS, SUMMED = 8, 7
PAIR = 2
STRIP = WIDTH // NZ
UNROLL = 4
MIX_ROWS = 768
N_SEND, N_RECV = 256, 256
members = ((1, 0), (0, 0), (2, 0), (0, 1), (3, 1), (1, 1), (2, 1), (3, 0))
ORDER = (
    (5, 0, 0, 3), (2, 0, 2), (2, 0, 0), (7, 1), (4, 0, 0, 0), (5, 0, 0, 2), (8, 1, 1, 1), (4, 0, 0, 1), (8, 1, 0, 1),
    (4, 0, 1, 0), (4, 0, 1, 1), (2, 0, 3), (2, 0, 1), (5, 0, 1, 2), (8, 1, 0, 2), (6, 1, 0, 0), (2, 1, 1), (0, 0),
    (2, 1, 0), (8, 1, 1, 2), (5, 0, 1, 3), (6, 1, 0, 1), (2, 1, 2), (3, 0, 0), (2, 1, 3), (7, 0), (8, 0, 1, 1),
    (8, 1, 0, 3), (8, 0, 0, 1), (3, 0, 2), (6, 2, 0, 0), (3, 0, 1), (6, 2, 0, 1), (8, 1, 1, 3), (3, 0, 3),
    (8, 0, 1, 2), (8, 1, 0, 4), (3, 1, 1), (7, 2), (8, 0, 0, 2), (6, 0, 1, 0), (8, 2, 1, 1), (0, 1), (8, 2, 0, 1),
    (3, 1, 2), (3, 1, 0), (3, 1, 3), (6, 0, 1, 1), (4, 1, 0, 0), (5, 1, 0, 3), (8, 0, 1, 3), (8, 2, 1, 2),
    (4, 1, 0, 1), (9, 1), (7, 3), (8, 3, 0, 1), (8, 2, 0, 2), (8, 0, 0, 3), (4, 1, 1, 0), (5, 1, 1, 2), (5, 1, 0, 2),
    (6, 1, 1, 0), (4, 1, 1, 1), (8, 3, 1, 1), (6, 3, 1, 0), (5, 1, 1, 3), (6, 1, 1, 1), (8, 0, 1, 4), (6, 3, 1, 1),
    (8, 2, 1, 3), (8, 3, 0, 2), (7, 5), (8, 5, 0, 1), (6, 3, 0, 1), (8, 5, 1, 1), (7, 4), (8, 2, 0, 3), (8, 3, 1, 2),
    (0, 2), (9, 0), (8, 4, 0, 1), (6, 2, 1, 0), (8, 4, 1, 1), (8, 3, 0, 3), (8, 2, 1, 4), (6, 2, 1, 1), (8, 5, 0, 2),
    (8, 5, 1, 2), (7, 6), (8, 6, 1, 1), (8, 6, 0, 1), (1,), (8, 3, 1, 3), (10, 1), (9, 2), (8, 3, 0, 4), (8, 4, 1, 2),
    (8, 5, 0, 3), (8, 4, 0, 2), (8, 6, 1, 2), (8, 5, 1, 3), (10, 0), (11, 1, 0, 2), (9, 3), (8, 5, 0, 4),
    (8, 6, 0, 2), (8, 4, 1, 3), (11, 1, 1, 2), (8, 6, 1, 3), (8, 4, 0, 3), (11, 1, 0, 3), (8, 4, 1, 4), (13, 7),
    (9, 5), (10, 2), (11, 0, 0, 2), (8, 6, 1, 4), (8, 6, 0, 3), (11, 0, 1, 2), (10, 3), (9, 4), (11, 7, 1, 2),
    (11, 0, 0, 3), (11, 7, 0, 2), (6, 3, 0, 0), (11, 2, 1, 2), (9, 6), (11, 1, 0, 4), (11, 1, 1, 3), (11, 0, 1, 3),
    (10, 5), (11, 2, 0, 2), (11, 3, 1, 2), (11, 7, 1, 3), (11, 3, 0, 2), (11, 7, 0, 3), (11, 2, 1, 3), (10, 4),
    (11, 5, 0, 2), (11, 0, 1, 4), (11, 3, 0, 3), (10, 6), (11, 5, 1, 2), (11, 4, 1, 2), (11, 3, 1, 3), (11, 5, 0, 3),
    (11, 4, 0, 2), (11, 7, 0, 4), (11, 6, 1, 2), (11, 2, 0, 3), (11, 6, 0, 2), (11, 2, 1, 4), (11, 4, 1, 3),
    (11, 3, 0, 4), (11, 5, 0, 4), (11, 6, 1, 3), (11, 4, 0, 3), (11, 5, 1, 3), (12, 1), (11, 4, 1, 4), (12, 7),
    (11, 6, 0, 3), (11, 6, 1, 4), (12, 0), (12, 2), (12, 3), (12, 5), (12, 4), (12, 6),
)


def rem(a, b):
    return lax.rem(a, jnp.int32(b))


def div(a, b):
    return lax.div(a, jnp.int32(b))


def slot_of(dx, dy, dc):
    return (dx * 2 + dy) * 2 + dc


def kernel(total_rows, total_cols, *refs):
    v_in, ham_in, nb_ref, out_ref = refs[:4]
    halos = refs[4:16]
    (v_ref, ham_ref, w1a, w1b, w2a, w2b, hown, hhalo, first, acc, panel, relay, ft, ssq, lz, ly, lx, lsum, lev,
     tpart, rs_in, rs_out, zsum, y_in, y_out, tfull, mixed, ssem, rsem, lsem) = refs[16:]
    w1, w2 = (w1a, w1b), (w2a, w2b)

    e = lax.axis_index("elem")
    o = lax.axis_index("orb")
    z, yl = rem(e, NZ), div(e, NZ)
    c, yh, x = rem(o, 2), rem(div(o, 2), 2), div(o, 4)
    y = yh * NY + yl
    xc = x * 2 + c

    def dev(x_, y_, z_, c_):
        return (rem(y_, NY) * NZ + z_, (x_ * 2 + div(y_, NY)) * 2 + c_)

    def zdev(j):
        return dev(x, y, rem(z + j, NZ), c)

    def ydev(j):
        return dev(x, rem(y + j, 2 * NY), z, c)

    def xdev(j):
        return dev(rem(x + j, NX), y, z, c)

    def xcdev(j):
        t = rem(xc + j, 2 * NX)
        return dev(div(t, 2), y, z, rem(t, 2))

    def mirror(j, dy, dc):
        return dev(rem(x + j, NX), rem(y + dy * NY, 2 * NY), z, c if dc == 0 else 1 - c)

    sibling = dev(x, y, z, 1 - c)
    tile_next = (rem(e + 1, NZ * NY), o)
    tile_prev = (rem(e + NZ * NY - 1, NZ * NY), o)

    counts = [0, 0]
    finals = []

    def ids(n=1):
        s = counts[0]
        counts[0] += n
        assert counts[0] <= N_SEND
        return s

    def copy(src, dst, send_id, recv_id, to):
        return pltpu.make_async_remote_copy(
            src_ref=src, dst_ref=dst, send_sem=ssem.at[send_id], recv_sem=rsem.at[recv_id],
            device_id=to, device_id_type=MESH)

    def push(src, dst, cid, to):
        d = copy(src, dst, cid, cid, to)
        d.start()
        finals.append(d.wait_send)

    def arrived(dst, cid):
        copy(dst, dst, cid, cid, sibling).wait_recv()

    load_v = pltpu.make_async_copy(v_in, v_ref, lsem.at[0])
    load_ham = pltpu.make_async_copy(ham_in, ham_ref, lsem.at[1])
    load_v.start()
    load_ham.start()

    barrier = pltpu.get_barrier_semaphore()
    peers = [tile_next, tile_prev]
    peers += [zdev(j) for j in range(1, NZ)]
    peers += [ydev(j) for j in range(1, 2 * NY)]
    peers += [xcdev(j) for j in range(1, 2 * NX)]
    for p in peers:
        pl.semaphore_signal(barrier, inc=1, device_id=p, device_id_type=MESH)
    pl.semaphore_wait(barrier, len(peers))

    def cols(h):
        return pl.ds(h * HALF, HALF)

    def halo(k, h, d):
        return halos[(k * 2 + h) * 2 + d]

    halo_id = [[[ids() for d in range(2)] for h in range(2)] for k in range(3)]

    def source(k, h):
        return v_ref.at[:, :, cols(h)] if k == 0 else (w1[h] if k == 1 else w2[h])

    def send_halo(k, h):
        push(source(k, h), halo(k, h, 0), halo_id[k][h][0], tile_next)
        push(source(k, h), halo(k, h, 1), halo_id[k][h][1], tile_prev)

    def loop(body):
        def step(t, carry):
            for u in range(UNROLL):
                body(t * UNROLL + u)
            return carry
        lax.fori_loop(0, TILE // UNROLL, step, 0)

    def block_of(i, n):
        return rem(nb_ref[n, i], TILE)

    def setup(i):
        hown[i] = jnp.concatenate([ham_ref[i, n] for n in range(5)], axis=1)
        hhalo[i] = jnp.concatenate([ham_ref[i, n] for n in range(5, 7)], axis=1)

    def own_part(k, h):
        def body(i):
            if k == 0:
                parts = [v_ref[block_of(i, n), :, cols(h)] for n in range(5)]
            else:
                parts = [(w1, w2)[k - 1][h][block_of(i, n)] for n in range(5)]
            acc[h, i] = jnp.dot(hown[i], jnp.concatenate(parts, axis=0), preferred_element_type=F32)
        loop(body)

    def finish(k, h):
        for d in range(2):
            arrived(halo(k, h, d), halo_id[k][h][d])

        def body(i):
            parts = [halo(k, h, d)[block_of(i, 5 + d)] for d in range(2)]
            t = acc[h, i] + jnp.dot(hhalo[i], jnp.concatenate(parts, axis=0), preferred_element_type=F32)
            if k == 0:
                first[h, i] = t
                w1[h][i] = t.astype(BF16)
            elif k == 1:
                w2[h][i] = (2.0 * t - v_ref[i, :, cols(h)].astype(F32)).astype(BF16)
            else:
                f = (2.0 * t - first[h, i]).astype(BF16)
                panel[0, pl.ds(pl.multiple_of(i * BLOCK, BLOCK), BLOCK), cols(h)] = f
                f = f.astype(F32)
                ssq[...] += jnp.sum((f * f).reshape(BLOCK // 8, 8, HALF), axis=0)
        loop(body)

    def piece(q, h, r):
        return panel.at[q, pl.ds(r * PIECE, PIECE), cols(h)]

    def half(q, h):
        return panel.at[q, :, cols(h)]

    pid = {}

    def pids(*key):
        if key not in pid:
            pid[key] = ids()
        return pid[key]

    def to_sibling(dx, dy, h):
        push(half(slot_of(dx, dy, 0), h), half(slot_of(dx, dy, 1), h), pids("s", dx, dy, h), sibling)

    def from_sibling(dx, dy, h):
        arrived(half(slot_of(dx, dy, 1), h), pids("s", dx, dy, h))

    def x_send(dy, h, r):
        push(piece(slot_of(0, dy, 0), h, r), piece(slot_of(3, dy, 0), h, r), pids("x", 3, dy, h, r), xdev(1))
        push(piece(slot_of(0, dy, 0), h, r), piece(slot_of(1, dy, 0), h, r), pids("x", 1, dy, h, r), xdev(NX - 1))

    def y_step(r):
        return ydev(2 if r in RIGHT else 2 * NY - 2)

    def y_send(h):
        for r in (0, 2, 1, 3):
            push(piece(0, h, r), relay.at[h, r], pids("y", h, r), y_step(r))

    def do_yr(h, r):
        arrived(relay.at[h, r], pids("y", h, r))
        push(relay.at[h, r], piece(slot_of(0, 1, 0), h, r), pids("Y", h, r), y_step(r))

    def do_par(h, r):
        arrived(piece(slot_of(0, 1, 0), h, r), pids("Y", h, r))
        x_send(1, h, r)

    def do_f3(dy, h, r):
        arrived(piece(slot_of(3, dy, 0), h, r), pids("x", 3, dy, h, r))
        push(piece(slot_of(3, dy, 0), h, r), piece(slot_of(2, dy, 0), h, r), pids("x", 2, dy, h, r), xdev(1))

    def do_f1(dy, h, r):
        arrived(piece(slot_of(1, dy, 0), h, r), pids("x", 1, dy, h, r))
        push(piece(slot_of(1, dy, 0), h, r), piece(slot_of(2, dy, 0), h, r), pids("x", 2, dy, h, r), xdev(NX - 1))

    def do_sib(dx, dy, h):
        for r in ((), RIGHT, RIGHT + LEFT, LEFT)[dx]:
            arrived(piece(slot_of(dx, dy, 0), h, r), pids("x", dx, dy, h, r))
        to_sibling(dx, dy, h)

    lev_id = [[ids() for j in range(8)] for s in range(3)]
    stages = ((lz, z, zdev), (ly, y, ydev), (lx, xc, xcdev))

    def do_ls(s):
        buf, me, to = stages[s]
        if s:
            prev, prev_me, _ = stages[s - 1]
            for j in range(1, 8):
                arrived(prev.at[rem(prev_me + 8 - j, 8)], lev_id[s - 1][j])
            value = jnp.sum(prev[...], axis=0)
        else:
            value = ssq[...]
        lsum[s] = value
        buf[me] = value
        for j in range(1, 8):
            push(lsum.at[s], buf.at[me], lev_id[s][j], to(j))

    def do_ld():
        for j in range(1, 8):
            arrived(lx.at[rem(xc + 8 - j, 8)], lev_id[2][j])
        total = jnp.sum(jnp.sum(lx[...], axis=0))
        level = jnp.full((8, HALF), total) / (total_cols * total_rows)
        lev[0] = level * total_rows
        lev[1] = jnp.sqrt(level)

    def slots(g):
        return [slot_of(*members[g], dc) for dc in range(PAIR)]

    def hops(g):
        return (3, 4) if g % 2 == 0 else (4, 3)

    def strip(d):
        return pl.ds(pl.multiple_of(d * STRIP, STRIP), STRIP)

    def pair(g):
        return pl.ds(slots(g)[0], PAIR)

    rs_id = [[[ids() for s in range(hops(g)[d])] for d in range(2)] for g in range(SUMMED)]
    ag_id = [[[ids() for s in range(hops(g)[d])] for d in range(2)] for g in range(GROUPS)]
    y_id = [[ids() for j in range(NY - 1)] for g in range(SUMMED)]
    mir_id = [[ids() for dc in range(PAIR)]]

    def along_z(d):
        return zdev(1 if d == 0 else NZ - 1)

    def do_gram(g):
        for h in range(2):
            from_sibling(*members[g], h)
        for q in slots(g):
            tpart[q] = jnp.dot(ft[...], panel[q], preferred_element_type=F32)

    def do_rs(g, d, s):
        ahead = hops(g)[d] - s + 1
        dest = rem(z + (ahead if d == 0 else NZ - ahead), NZ)
        value = tpart[pair(g), strip(dest), :]
        if s > 1:
            arrived(rs_in.at[g, d, s - 2], rs_id[g][d][s - 2])
            value = value + rs_in[g, d, s - 2].astype(F32)
        rs_out[g, d, s - 1] = value.astype(BF16)
        push(rs_out.at[g, d, s - 1], rs_in.at[g, d, s - 1], rs_id[g][d][s - 1], along_z(d))

    def do_rsd(g):
        value = tpart[pair(g), strip(z), :]
        for d in range(2):
            n = hops(g)[d]
            arrived(rs_in.at[g, d, n - 1], rs_id[g][d][n - 1])
            value = value + rs_in[g, d, n - 1].astype(F32)
        zsum[g] = value
        y_out[g] = value.astype(BF16)
        for j in range(1, NY):
            push(y_out.at[g], y_in.at[g, j - 1], y_id[g][j - 1], dev(x, yh * NY + rem(yl + j, NY), z, c))

    def region(g, d):
        return tfull.at[pair(g), strip(d), :]

    def ag_send(g, d, s):
        behind = rem(z + ((NZ - s + 1) if d == 0 else (s - 1)), NZ)
        if s > 1:
            arrived(region(g, behind), ag_id[g][d][s - 2])
        push(region(g, behind), region(g, behind), ag_id[g][d][s - 1], along_z(d))

    def do_sc(g):
        value = zsum[g]
        for j in range(NY - 1):
            arrived(y_in.at[g, j], y_id[g][j])
            value = value + y_in[g, j].astype(F32)
        value = value / jnp.max(lev[0])
        tfull[pair(g), strip(z), :] = value.astype(BF16)
        for d in range(2):
            ag_send(g, d, 1)
        dx, dy = members[g]
        if (dx, dy) == (1, 0):
            for dc in range(PAIR):
                push(tfull.at[slot_of(1, dy, dc), strip(z), :], tfull.at[slot_of(3, dy, dc), strip(z), :],
                     mir_id[dy][dc], mirror(1, dy, dc))

    def do_mir(g):
        dx, dy = members[g]
        for dc in range(PAIR):
            arrived(tfull.at[slot_of(3, dy, dc), strip(z), :], mir_id[dy][dc])
        for d in range(2):
            ag_send(g, d, 1)

    do_ag = ag_send

    def do_mix(g):
        for d in range(2):
            n = hops(g)[d]
            arrived(region(g, rem(z + (NZ - n if d == 0 else n), NZ)), ag_id[g][d][n - 1])
        initial, final = g == mixes[0], g == mixes[-1]

        mirrored = members[g] == (3, 0)
        if mirrored:
            for h in range(2):
                from_sibling(*members[g], h)
        side = 0 if mirrored else 1
        strips = jnp.concatenate([tfull[q] for q in slots(g)], axis=side)
        for t in range(ROWS // MIX_ROWS):
            rows = pl.ds(t * MIX_ROWS, MIX_ROWS)
            left = jnp.concatenate([panel[q, rows, :] for q in slots(g)], axis=1)
            value = lax.dot_general(left, strips, (((1,), (side,)), ((), ())), preferred_element_type=F32)
            if not initial:
                value = value + mixed[rows, :]
            if final:
                f = panel[0, rows, :].astype(F32)
                out_ref[rows, :] = ((1.5 * f - 0.5 * value) / jnp.max(lev[1])).astype(BF16)
            else:
                mixed[rows, :] = value

    def transposed(h):
        ft[pl.ds(h * HALF, HALF), :] = panel[0, :, cols(h)].T

    def launch(h):
        y_send(h)
        for r in (0, 2, 1, 3):
            x_send(0, h, r)
        to_sibling(0, 0, h)
        transposed(h)

    load_v.wait()
    send_halo(0, 0)
    send_halo(0, 1)
    ssq[...] = jnp.zeros_like(ssq)
    load_ham.wait()
    loop(setup)
    own_part(0, 0)
    own_part(0, 1)
    for k in range(3):
        for h in range(2):
            finish(k, h)
            if k < 2:
                send_halo(k + 1, h)
                own_part(k + 1, h)
            else:
                launch(h)

    steps = (do_ls, do_ld, do_yr, do_par, do_f3, do_f1, do_sib, do_gram, do_rs, do_rsd, do_sc, do_ag, do_mix, do_mir)
    mixes = [numbers[0] for kind, *numbers in ORDER if steps[kind] is do_mix]
    for kind, *numbers in ORDER:
        steps[kind](*numbers)
    for fn in finals:
        fn()


def solution(mesh):
    sizes = dict(mesh.shape)

    def local(orbitals, hamiltonian, neighbours):
        rows, width = orbitals.shape
        total_rows, total_cols = rows * sizes["elem"], width * sizes["orb"]
        assert (rows, width) == (ROWS, WIDTH)
        vmem = pl.BlockSpec(memory_space=pltpu.VMEM)
        anywhere = pl.BlockSpec(memory_space=pl.ANY)
        block = pltpu.VMEM((TILE, BLOCK, HALF), BF16)
        return pl.pallas_call(
            lambda *refs: kernel(total_rows, total_cols, *refs),
            out_shape=jax.ShapeDtypeStruct((rows, width), BF16),
            in_specs=[anywhere, anywhere, pl.BlockSpec(memory_space=pltpu.SMEM)],
            out_specs=vmem,
            scratch_shapes=[block] * 12 + [
                pltpu.VMEM((TILE, BLOCK, WIDTH), BF16),
                pltpu.VMEM(hamiltonian.shape, BF16),
            ] + [block] * 4 + [
                pltpu.VMEM((TILE, BLOCK, 5 * BLOCK), BF16),
                pltpu.VMEM((TILE, BLOCK, 2 * BLOCK), BF16),
                pltpu.VMEM((2, TILE, BLOCK, HALF), F32),
                pltpu.VMEM((2, TILE, BLOCK, HALF), F32),
                pltpu.VMEM((SLOTS, ROWS, WIDTH), BF16),
                pltpu.VMEM((2, PIECES, PIECE, HALF), BF16),
                pltpu.VMEM((WIDTH, ROWS), BF16),
                pltpu.VMEM((8, HALF), F32),
                pltpu.VMEM((8, 8, HALF), F32),
                pltpu.VMEM((8, 8, HALF), F32),
                pltpu.VMEM((8, 8, HALF), F32),
                pltpu.VMEM((3, 8, HALF), F32),
                pltpu.VMEM((2, 8, HALF), F32),
                pltpu.VMEM((SLOTS, WIDTH, WIDTH), F32),
                pltpu.VMEM((GROUPS, 2, 4, PAIR, STRIP, WIDTH), BF16),
                pltpu.VMEM((GROUPS, 2, 4, PAIR, STRIP, WIDTH), BF16),
                pltpu.VMEM((GROUPS, PAIR, STRIP, WIDTH), F32),
                pltpu.VMEM((GROUPS, NY - 1, PAIR, STRIP, WIDTH), BF16),
                pltpu.VMEM((GROUPS, PAIR, STRIP, WIDTH), BF16),
                pltpu.VMEM((SLOTS, WIDTH, WIDTH), BF16),
                pltpu.VMEM((ROWS, WIDTH), F32),
                pltpu.SemaphoreType.DMA((N_SEND,)),
                pltpu.SemaphoreType.DMA((N_RECV,)),
                pltpu.SemaphoreType.DMA((2,)),
            ],
            compiler_params=pltpu.CompilerParams(
                collective_id=0, has_side_effects=True, vmem_limit_bytes=56 * 1024 * 1024),
            name="filter_gram",
        )(orbitals.reshape(TILE, BLOCK, width), hamiltonian, neighbours.T)

    return jax.shard_map(
        local,
        mesh=mesh,
        in_specs=(P("elem", "orb"), P("elem", None, None, None), P("elem", None)),
        out_specs=P("elem", "orb"),
        check_vma=False,
    )
```

```python
import jax
import jax.numpy as jnp
from jax import lax
from jax.experimental import pallas as pl
from jax.experimental.pallas import tpu as pltpu
from jax.sharding import PartitionSpec as P

MESH = pl.DeviceIdType.MESH
F32 = jnp.float32
BF16 = jnp.bfloat16
NX, NY, NZ = 4, 4, 8
TILE, BLOCK, WIDTH, HALF = 12, 64, 256, 128
ROWS = TILE * BLOCK
PIECES = 4
PIECE = ROWS // PIECES
RIGHT, LEFT = (0, 1), (2, 3)
SLOTS = 16
GROUPS, SUMMED = 8, 7
PAIR = 2
STRIP = WIDTH // NZ
UNROLL = 4
MIX_ROWS = 768
N_SEND, N_RECV = 256, 256
members = ((1, 0), (0, 0), (2, 0), (0, 1), (3, 1), (1, 1), (2, 1), (3, 0))
ORDER = (
    (5, 0, 0, 3), (2, 0, 2), (2, 0, 0), (7, 1), (4, 0, 0, 0), (5, 0, 0, 2), (8, 1, 1, 1), (4, 0, 0, 1), (8, 1, 0, 1),
    (4, 0, 1, 0), (4, 0, 1, 1), (2, 0, 3), (2, 0, 1), (5, 0, 1, 2), (8, 1, 0, 2), (6, 1, 0, 0), (2, 1, 1), (0, 0),
    (2, 1, 0), (8, 1, 1, 2), (5, 0, 1, 3), (6, 1, 0, 1), (2, 1, 2), (3, 0, 0), (2, 1, 3), (7, 0), (8, 0, 1, 1),
    (8, 1, 0, 3), (8, 0, 0, 1), (3, 0, 2), (6, 2, 0, 0), (3, 0, 1), (6, 2, 0, 1), (8, 1, 1, 3), (3, 0, 3),
    (8, 0, 1, 2), (8, 1, 0, 4), (3, 1, 1), (7, 2), (8, 0, 0, 2), (6, 0, 1, 0), (8, 2, 1, 1), (0, 1), (8, 2, 0, 1),
    (3, 1, 2), (3, 1, 0), (3, 1, 3), (6, 0, 1, 1), (4, 1, 0, 0), (5, 1, 0, 3), (8, 0, 1, 3), (8, 2, 1, 2),
    (4, 1, 0, 1), (9, 1), (7, 3), (8, 3, 0, 1), (8, 2, 0, 2), (8, 0, 0, 3), (4, 1, 1, 0), (5, 1, 1, 2), (5, 1, 0, 2),
    (6, 1, 1, 0), (4, 1, 1, 1), (8, 3, 1, 1), (6, 3, 1, 0), (5, 1, 1, 3), (6, 1, 1, 1), (8, 0, 1, 4), (6, 3, 1, 1),
    (8, 2, 1, 3), (8, 3, 0, 2), (7, 5), (8, 5, 0, 1), (6, 3, 0, 1), (8, 5, 1, 1), (7, 4), (8, 2, 0, 3), (8, 3, 1, 2),
    (0, 2), (9, 0), (8, 4, 0, 1), (6, 2, 1, 0), (8, 4, 1, 1), (8, 3, 0, 3), (8, 2, 1, 4), (6, 2, 1, 1), (8, 5, 0, 2),
    (8, 5, 1, 2), (7, 6), (8, 6, 1, 1), (8, 6, 0, 1), (1,), (8, 3, 1, 3), (10, 1), (9, 2), (8, 3, 0, 4), (8, 4, 1, 2),
    (8, 5, 0, 3), (8, 4, 0, 2), (8, 6, 1, 2), (8, 5, 1, 3), (10, 0), (11, 1, 0, 2), (9, 3), (8, 5, 0, 4),
    (8, 6, 0, 2), (8, 4, 1, 3), (11, 1, 1, 2), (8, 6, 1, 3), (8, 4, 0, 3), (11, 1, 0, 3), (8, 4, 1, 4), (13, 7),
    (9, 5), (10, 2), (11, 0, 0, 2), (8, 6, 1, 4), (8, 6, 0, 3), (11, 0, 1, 2), (10, 3), (9, 4), (11, 7, 1, 2),
    (11, 0, 0, 3), (11, 7, 0, 2), (6, 3, 0, 0), (11, 2, 1, 2), (9, 6), (11, 1, 0, 4), (11, 1, 1, 3), (11, 0, 1, 3),
    (10, 5), (11, 2, 0, 2), (11, 3, 1, 2), (11, 7, 1, 3), (11, 3, 0, 2), (11, 7, 0, 3), (11, 2, 1, 3), (10, 4),
    (11, 5, 0, 2), (11, 0, 1, 4), (11, 3, 0, 3), (10, 6), (11, 5, 1, 2), (11, 4, 1, 2), (11, 3, 1, 3), (11, 5, 0, 3),
    (11, 4, 0, 2), (11, 7, 0, 4), (11, 6, 1, 2), (11, 2, 0, 3), (11, 6, 0, 2), (11, 2, 1, 4), (11, 4, 1, 3),
    (11, 3, 0, 4), (11, 5, 0, 4), (11, 6, 1, 3), (11, 4, 0, 3), (11, 5, 1, 3), (12, 1), (11, 4, 1, 4), (12, 7),
    (11, 6, 0, 3), (11, 6, 1, 4), (12, 0), (12, 2), (12, 3), (12, 5), (12, 4), (12, 6),
)


def rem(a, b):
    return lax.rem(a, jnp.int32(b))


def div(a, b):
    return lax.div(a, jnp.int32(b))


def slot_of(dx, dy, dc):
    return (dx * 2 + dy) * 2 + dc


def kernel(total_rows, total_cols, *refs):
    v_in, ham_in, nb_ref, out_ref = refs[:4]
    halos = refs[4:16]
    (v_ref, ham_ref, w1a, w1b, w2a, w2b, hown, hhalo, first, acc, panel, relay, ft, ssq, lz, ly, lx, lsum, lev,
     tpart, rs_in, rs_out, zsum, y_in, y_out, tfull, mixed, ssem, rsem, lsem) = refs[16:]
    w1, w2 = (w1a, w1b), (w2a, w2b)

    e = lax.axis_index("elem")
    o = lax.axis_index("orb")
    z, yl = rem(e, NZ), div(e, NZ)
    c, yh, x = rem(o, 2), rem(div(o, 2), 2), div(o, 4)
    y = yh * NY + yl
    xc = x * 2 + c

    def dev(x_, y_, z_, c_):
        return (rem(y_, NY) * NZ + z_, (x_ * 2 + div(y_, NY)) * 2 + c_)

    def zdev(j):
        return dev(x, y, rem(z + j, NZ), c)

    def ydev(j):
        return dev(x, rem(y + j, 2 * NY), z, c)

    def xdev(j):
        return dev(rem(x + j, NX), y, z, c)

    def xcdev(j):
        t = rem(xc + j, 2 * NX)
        return dev(div(t, 2), y, z, rem(t, 2))

    def mirror(j, dy, dc):
        return dev(rem(x + j, NX), rem(y + dy * NY, 2 * NY), z, c if dc == 0 else 1 - c)

    sibling = dev(x, y, z, 1 - c)
    tile_next = (rem(e + 1, NZ * NY), o)
    tile_prev = (rem(e + NZ * NY - 1, NZ * NY), o)

    counts = [0, 0]
    finals = []

    def ids(n=1):
        s = counts[0]
        counts[0] += n
        assert counts[0] <= N_SEND
        return s

    def copy(src, dst, send_id, recv_id, to):
        return pltpu.make_async_remote_copy(
            src_ref=src, dst_ref=dst, send_sem=ssem.at[send_id], recv_sem=rsem.at[recv_id],
            device_id=to, device_id_type=MESH)

    def push(src, dst, cid, to):
        d = copy(src, dst, cid, cid, to)
        d.start()
        finals.append(d.wait_send)

    def arrived(dst, cid):
        copy(dst, dst, cid, cid, sibling).wait_recv()

    load_v = pltpu.make_async_copy(v_in, v_ref, lsem.at[0])
    load_ham = pltpu.make_async_copy(ham_in, ham_ref, lsem.at[1])
    load_v.start()
    load_ham.start()

    barrier = pltpu.get_barrier_semaphore()
    peers = [tile_next, tile_prev]
    peers += [zdev(j) for j in range(1, NZ)]
    peers += [ydev(j) for j in range(1, 2 * NY)]
    peers += [xcdev(j) for j in range(1, 2 * NX)]
    for p in peers:
        pl.semaphore_signal(barrier, inc=1, device_id=p, device_id_type=MESH)
    pl.semaphore_wait(barrier, len(peers))

    def cols(h):
        return pl.ds(h * HALF, HALF)

    def halo(k, h, d):
        return halos[(k * 2 + h) * 2 + d]

    halo_id = [[[ids() for d in range(2)] for h in range(2)] for k in range(3)]

    def source(k, h):
        return v_ref.at[:, :, cols(h)] if k == 0 else (w1[h] if k == 1 else w2[h])

    def send_halo(k, h):
        push(source(k, h), halo(k, h, 0), halo_id[k][h][0], tile_next)
        push(source(k, h), halo(k, h, 1), halo_id[k][h][1], tile_prev)

    def loop(body):
        def step(t, carry):
            for u in range(UNROLL):
                body(t * UNROLL + u)
            return carry
        lax.fori_loop(0, TILE // UNROLL, step, 0)

    def block_of(i, n):
        return rem(nb_ref[n, i], TILE)

    def setup(i):
        hown[i] = jnp.concatenate([ham_ref[i, n] for n in range(5)], axis=1)
        hhalo[i] = jnp.concatenate([ham_ref[i, n] for n in range(5, 7)], axis=1)

    def own_part(k, h):
        def body(i):
            if k == 0:
                parts = [v_ref[block_of(i, n), :, cols(h)] for n in range(5)]
            else:
                parts = [(w1, w2)[k - 1][h][block_of(i, n)] for n in range(5)]
            acc[h, i] = jnp.dot(hown[i], jnp.concatenate(parts, axis=0), preferred_element_type=F32)
        loop(body)

    def finish(k, h):
        for d in range(2):
            arrived(halo(k, h, d), halo_id[k][h][d])

        def body(i):
            parts = [halo(k, h, d)[block_of(i, 5 + d)] for d in range(2)]
            t = acc[h, i] + jnp.dot(hhalo[i], jnp.concatenate(parts, axis=0), preferred_element_type=F32)
            if k == 0:
                first[h, i] = t
                w1[h][i] = t.astype(BF16)
            elif k == 1:
                w2[h][i] = (2.0 * t - v_ref[i, :, cols(h)].astype(F32)).astype(BF16)
            else:
                f = (2.0 * t - first[h, i]).astype(BF16)
                panel[0, pl.ds(pl.multiple_of(i * BLOCK, BLOCK), BLOCK), cols(h)] = f
                f = f.astype(F32)
                ssq[...] += jnp.sum((f * f).reshape(BLOCK // 8, 8, HALF), axis=0)
        loop(body)

    def piece(q, h, r):
        return panel.at[q, pl.ds(r * PIECE, PIECE), cols(h)]

    def half(q, h):
        return panel.at[q, :, cols(h)]

    pid = {}

    def pids(*key):
        if key not in pid:
            pid[key] = ids()
        return pid[key]

    def to_sibling(dx, dy, h):
        push(half(slot_of(dx, dy, 0), h), half(slot_of(dx, dy, 1), h), pids("s", dx, dy, h), sibling)

    def from_sibling(dx, dy, h):
        arrived(half(slot_of(dx, dy, 1), h), pids("s", dx, dy, h))

    def x_send(dy, h, r):
        push(piece(slot_of(0, dy, 0), h, r), piece(slot_of(3, dy, 0), h, r), pids("x", 3, dy, h, r), xdev(1))
        push(piece(slot_of(0, dy, 0), h, r), piece(slot_of(1, dy, 0), h, r), pids("x", 1, dy, h, r), xdev(NX - 1))

    def y_step(r):
        return ydev(2 if r in RIGHT else 2 * NY - 2)

    def y_send(h):
        for r in (0, 2, 1, 3):
            push(piece(0, h, r), relay.at[h, r], pids("y", h, r), y_step(r))

    def do_yr(h, r):
        arrived(relay.at[h, r], pids("y", h, r))
        push(relay.at[h, r], piece(slot_of(0, 1, 0), h, r), pids("Y", h, r), y_step(r))

    def do_par(h, r):
        arrived(piece(slot_of(0, 1, 0), h, r), pids("Y", h, r))
        x_send(1, h, r)

    def do_f3(dy, h, r):
        arrived(piece(slot_of(3, dy, 0), h, r), pids("x", 3, dy, h, r))
        push(piece(slot_of(3, dy, 0), h, r), piece(slot_of(2, dy, 0), h, r), pids("x", 2, dy, h, r), xdev(1))

    def do_f1(dy, h, r):
        arrived(piece(slot_of(1, dy, 0), h, r), pids("x", 1, dy, h, r))
        push(piece(slot_of(1, dy, 0), h, r), piece(slot_of(2, dy, 0), h, r), pids("x", 2, dy, h, r), xdev(NX - 1))

    def do_sib(dx, dy, h):
        for r in ((), RIGHT, RIGHT + LEFT, LEFT)[dx]:
            arrived(piece(slot_of(dx, dy, 0), h, r), pids("x", dx, dy, h, r))
        to_sibling(dx, dy, h)

    lev_id = [[ids() for j in range(8)] for s in range(3)]
    stages = ((lz, z, zdev), (ly, y, ydev), (lx, xc, xcdev))

    def do_ls(s):
        buf, me, to = stages[s]
        if s:
            prev, prev_me, _ = stages[s - 1]
            for j in range(1, 8):
                arrived(prev.at[rem(prev_me + 8 - j, 8)], lev_id[s - 1][j])
            value = jnp.sum(prev[...], axis=0)
        else:
            value = ssq[...]
        lsum[s] = value
        buf[me] = value
        for j in range(1, 8):
            push(lsum.at[s], buf.at[me], lev_id[s][j], to(j))

    def do_ld():
        for j in range(1, 8):
            arrived(lx.at[rem(xc + 8 - j, 8)], lev_id[2][j])
        total = jnp.sum(jnp.sum(lx[...], axis=0))
        level = jnp.full((8, HALF), total) / (total_cols * total_rows)
        lev[0] = level * total_rows
        lev[1] = 1.0 / jnp.sqrt(level)

    def slots(g):
        return [slot_of(*members[g], dc) for dc in range(PAIR)]

    def hops(g):
        return (3, 4) if g % 2 == 0 else (4, 3)

    def strip(d):
        return pl.ds(pl.multiple_of(d * STRIP, STRIP), STRIP)

    def pair(g):
        return pl.ds(slots(g)[0], PAIR)

    rs_id = [[[ids() for s in range(hops(g)[d])] for d in range(2)] for g in range(SUMMED)]
    ag_id = [[[ids() for s in range(hops(g)[d])] for d in range(2)] for g in range(GROUPS)]
    y_id = [[ids() for j in range(NY - 1)] for g in range(SUMMED)]
    mir_id = [[ids() for dc in range(PAIR)]]

    def along_z(d):
        return zdev(1 if d == 0 else NZ - 1)

    def do_gram(g):
        for h in range(2):
            from_sibling(*members[g], h)
        for q in slots(g):
            tpart[q] = jnp.dot(ft[...], panel[q], preferred_element_type=F32)

    def do_rs(g, d, s):
        ahead = hops(g)[d] - s + 1
        dest = rem(z + (ahead if d == 0 else NZ - ahead), NZ)
        value = tpart[pair(g), strip(dest), :]
        if s > 1:
            arrived(rs_in.at[g, d, s - 2], rs_id[g][d][s - 2])
            value = value + rs_in[g, d, s - 2].astype(F32)
        rs_out[g, d, s - 1] = value.astype(BF16)
        push(rs_out.at[g, d, s - 1], rs_in.at[g, d, s - 1], rs_id[g][d][s - 1], along_z(d))

    def do_rsd(g):
        value = tpart[pair(g), strip(z), :]
        for d in range(2):
            n = hops(g)[d]
            arrived(rs_in.at[g, d, n - 1], rs_id[g][d][n - 1])
            value = value + rs_in[g, d, n - 1].astype(F32)
        zsum[g] = value
        y_out[g] = value.astype(BF16)
        for j in range(1, NY):
            push(y_out.at[g], y_in.at[g, j - 1], y_id[g][j - 1], dev(x, yh * NY + rem(yl + j, NY), z, c))

    def region(g, d):
        return tfull.at[pair(g), strip(d), :]

    def ag_send(g, d, s):
        behind = rem(z + ((NZ - s + 1) if d == 0 else (s - 1)), NZ)
        if s > 1:
            arrived(region(g, behind), ag_id[g][d][s - 2])
        push(region(g, behind), region(g, behind), ag_id[g][d][s - 1], along_z(d))

    def do_sc(g):
        value = zsum[g]
        for j in range(NY - 1):
            arrived(y_in.at[g, j], y_id[g][j])
            value = value + y_in[g, j].astype(F32)
        value = value / jnp.max(lev[0])
        tfull[pair(g), strip(z), :] = value.astype(BF16)
        for d in range(2):
            ag_send(g, d, 1)
        dx, dy = members[g]
        if (dx, dy) == (1, 0):
            for dc in range(PAIR):
                push(tfull.at[slot_of(1, dy, dc), strip(z), :], tfull.at[slot_of(3, dy, dc), strip(z), :],
                     mir_id[dy][dc], mirror(1, dy, dc))

    def do_mir(g):
        dx, dy = members[g]
        for dc in range(PAIR):
            arrived(tfull.at[slot_of(3, dy, dc), strip(z), :], mir_id[dy][dc])
        for d in range(2):
            ag_send(g, d, 1)

    do_ag = ag_send

    def do_mix(g):
        for d in range(2):
            n = hops(g)[d]
            arrived(region(g, rem(z + (NZ - n if d == 0 else n), NZ)), ag_id[g][d][n - 1])
        initial, final = g == mixes[0], g == mixes[-1]

        mirrored = members[g] == (3, 0)
        if mirrored:
            for h in range(2):
                from_sibling(*members[g], h)
        side = 0 if mirrored else 1
        strips = jnp.concatenate([tfull[q] for q in slots(g)], axis=side)
        for t in range(ROWS // MIX_ROWS):
            rows = pl.ds(t * MIX_ROWS, MIX_ROWS)
            left = jnp.concatenate([panel[q, rows, :] for q in slots(g)], axis=1)
            value = lax.dot_general(left, strips, (((1,), (side,)), ((), ())), preferred_element_type=F32)
            if not initial:
                value = value + mixed[rows, :]
            if final:
                f = panel[0, rows, :].astype(F32)
                out_ref[rows, :] = ((1.5 * f - 0.5 * value) * jnp.max(lev[1])).astype(BF16)
            else:
                mixed[rows, :] = value

    def transposed(h):
        ft[pl.ds(h * HALF, HALF), :] = panel[0, :, cols(h)].T

    def launch(h):
        y_send(h)
        for r in (0, 2, 1, 3):
            x_send(0, h, r)
        to_sibling(0, 0, h)
        transposed(h)

    load_v.wait()
    send_halo(0, 0)
    send_halo(0, 1)
    ssq[...] = jnp.zeros_like(ssq)
    load_ham.wait()
    loop(setup)
    own_part(0, 0)
    own_part(0, 1)
    for k in range(3):
        for h in range(2):
            finish(k, h)
            if k < 2:
                send_halo(k + 1, h)
                own_part(k + 1, h)
            else:
                launch(h)

    steps = (do_ls, do_ld, do_yr, do_par, do_f3, do_f1, do_sib, do_gram, do_rs, do_rsd, do_sc, do_ag, do_mix, do_mir)
    mixes = [numbers[0] for kind, *numbers in ORDER if steps[kind] is do_mix]
    settled = 0
    for n, (kind, *numbers) in enumerate(ORDER):
        if n == len(ORDER) - 40:
            settled = len(finals)
        if n == len(ORDER) - 1:
            for fn in finals[:settled]:
                fn()
            del finals[:settled]
        steps[kind](*numbers)
    for fn in finals:
        fn()


def solution(mesh):
    sizes = dict(mesh.shape)

    def local(orbitals, hamiltonian, neighbours):
        rows, width = orbitals.shape
        total_rows, total_cols = rows * sizes["elem"], width * sizes["orb"]
        assert (rows, width) == (ROWS, WIDTH)
        vmem = pl.BlockSpec(memory_space=pltpu.VMEM)
        anywhere = pl.BlockSpec(memory_space=pl.ANY)
        block = pltpu.VMEM((TILE, BLOCK, HALF), BF16)
        return pl.pallas_call(
            lambda *refs: kernel(total_rows, total_cols, *refs),
            out_shape=jax.ShapeDtypeStruct((rows, width), BF16),
            in_specs=[anywhere, anywhere, pl.BlockSpec(memory_space=pltpu.SMEM)],
            out_specs=vmem,
            scratch_shapes=[block] * 12 + [
                pltpu.VMEM((TILE, BLOCK, WIDTH), BF16),
                pltpu.VMEM(hamiltonian.shape, BF16),
            ] + [block] * 4 + [
                pltpu.VMEM((TILE, BLOCK, 5 * BLOCK), BF16),
                pltpu.VMEM((TILE, BLOCK, 2 * BLOCK), BF16),
                pltpu.VMEM((2, TILE, BLOCK, HALF), F32),
                pltpu.VMEM((2, TILE, BLOCK, HALF), F32),
                pltpu.VMEM((SLOTS, ROWS, WIDTH), BF16),
                pltpu.VMEM((2, PIECES, PIECE, HALF), BF16),
                pltpu.VMEM((WIDTH, ROWS), BF16),
                pltpu.VMEM((8, HALF), F32),
                pltpu.VMEM((8, 8, HALF), F32),
                pltpu.VMEM((8, 8, HALF), F32),
                pltpu.VMEM((8, 8, HALF), F32),
                pltpu.VMEM((3, 8, HALF), F32),
                pltpu.VMEM((2, 8, HALF), F32),
                pltpu.VMEM((SLOTS, WIDTH, WIDTH), F32),
                pltpu.VMEM((GROUPS, 2, 4, PAIR, STRIP, WIDTH), BF16),
                pltpu.VMEM((GROUPS, 2, 4, PAIR, STRIP, WIDTH), BF16),
                pltpu.VMEM((GROUPS, PAIR, STRIP, WIDTH), F32),
                pltpu.VMEM((GROUPS, NY - 1, PAIR, STRIP, WIDTH), BF16),
                pltpu.VMEM((GROUPS, PAIR, STRIP, WIDTH), BF16),
                pltpu.VMEM((SLOTS, WIDTH, WIDTH), BF16),
                pltpu.VMEM((ROWS, WIDTH), F32),
                pltpu.SemaphoreType.DMA((N_SEND,)),
                pltpu.SemaphoreType.DMA((N_RECV,)),
                pltpu.SemaphoreType.DMA((2,)),
            ],
            compiler_params=pltpu.CompilerParams(
                collective_id=0, has_side_effects=True, vmem_limit_bytes=56 * 1024 * 1024),
            name="filter_gram",
        )(orbitals.reshape(TILE, BLOCK, width), hamiltonian, neighbours.T)

    return jax.shard_map(
        local,
        mesh=mesh,
        in_specs=(P("elem", "orb"), P("elem", None, None, None), P("elem", None)),
        out_specs=P("elem", "orb"),
        check_vma=False,
    )
```
